32 devices in a mesh: parts: 2 (over y), bank: 8 (over z, x), batch: 2 (over core).
Axes of the slice: x: 2, y: 2, z: 4, core: 2. Of those that a mesh axis runs over, the one named last changes fastest.
Arguments:
- bank: bfloat16 [32768, 256], P(('parts', 'bank')), parts along dimension 0, may hold values from -1 to 1
- queries: bfloat16 [4096, 256], P(('parts', 'batch')), parts along dimension 0, may hold values from -8 to 8
- keys: bfloat16 [4096, 256], P(('parts', 'batch')), parts along dimension 0, may hold values from -0.375 to 0.375
- labels: int32 [4096], P(('parts', 'batch')), parts along dimension 0, may hold values from 0 to 2047, each once
- mask_tiles: int32 [32, 16], P('parts'), parts along dimension 0, may hold values from 0 to 127
Outputs:
- new_bank: bfloat16 [32768, 256], P(('parts', 'bank')), parts along dimension 0
- query_grad: float32 [4096, 256], P(('parts', 'batch')), parts along dimension 0
- loss: float32 [4096], P(('parts', 'batch')), parts along dimension 0
The draws below stay inside these ranges and needn't reach their ends.
There are 2 independent parts, one for each index of `parts`. The reference program is written for one: setup_inputs(seed, part) draws one part's arguments, and reference() takes and returns one part's arrays. A program takes and returns all parts, laid end to end along the dimension named above; each array names one. Nothing has to cross between parts.
Inputs may be any that keep to these rules, and one draw needn't show every extreme that they name: `labels`: a permutation: each row of keys is the positive of exactly one query. `mask_tiles`: tile t holds bank rows t * 128 to t * 128 + 127; row b lists tiles excluded for queries b * 128 to b * 128 + 127; numbers may repeat.
All inputs are finite; a program needn't handle non-finite values.
Results may differ from the reference program's by a relative error of at most 0.0055.
Values may be sent and summed in bfloat16 or wider, within the bound.
A program may use at most 64 MiB of HBM per device.

```python
import math
import jax
import jax.numpy as jnp
from jax import lax

D = 256
TILE = 128
BANK = 16384
QUERIES = 2048
QBLK = 16
KT = 128
MB = 16


def draw_bank(key, part):
    k_base = jax.random.fold_in(jax.random.fold_in(key, 1), 0)
    ramp = 0.75 + 0.5 * jnp.arange(BANK, dtype=jnp.float32) / BANK
    base = jax.random.truncated_normal(k_base, -6.0, 6.0, (BANK, D), jnp.float32) * ramp[:, None] * D ** (-0.5)
    return base.astype(jnp.bfloat16)


def draw_queries(key, part):
    k_base = jax.random.fold_in(jax.random.fold_in(key, 2), 0)
    base = 0.35 * jax.random.truncated_normal(k_base, -6.0, 6.0, (QUERIES, D), jnp.float32)
    return base.astype(jnp.bfloat16)


def touch_ends(array, key, smallest, largest):
    longest = array.shape.index(max(array.shape))
    spots = []
    for shift in (0, 1):
        where = [jax.random.randint(jax.random.fold_in(key, axis), (), 0, length) for axis, length in enumerate(array.shape)]
        where[longest] = (where[longest] + shift) % array.shape[longest]
        spots.append(tuple(where))
    return array.at[spots[0]].set(smallest).at[spots[1]].set(largest)


def level_of(own_key, shape, cuts, smallest, largest):
    gain, own = 1.0, jax.random.fold_in(own_key, 6)
    for dim, parts in cuts:
        steps = jnp.exp(jax.random.uniform(jax.random.fold_in(own, dim), (parts,), jnp.float32, smallest / len(cuts), largest / len(cuts)))
        gain = gain * jnp.repeat(steps, shape[dim] // parts).reshape([-1 if axis == dim else 1 for axis in range(len(shape))])
    return gain


def noise(own_key, extent, deviation, most, cuts=(), kind=jnp.bfloat16):
    level = level_of(own_key, extent, cuts, -0.22, 0.18) if cuts else 1.0
    result = jax.random.normal(own_key, extent, jnp.float32) * deviation * level
    return jnp.minimum(jnp.maximum(result, -most), most).astype(kind)


def setup_inputs(seed: int = 0, part: int = 0) -> dict:
    arg_keys = jax.random.split(jax.random.key(seed), 6)
    part_splits = jax.random.split(jax.random.fold_in(arg_keys[5], part), 6)
    bank = draw_bank(jax.random.fold_in(jax.random.fold_in(arg_keys[5], part), 71), part)
    queries = draw_queries(jax.random.fold_in(jax.random.fold_in(arg_keys[5], part), 71), part)
    keys = noise(part_splits[2], (QUERIES, D), (D ** -0.5), 0.375, ((0, 2),))
    labels = jax.random.permutation(part_splits[3], QUERIES).astype(jnp.int32)
    mask_tiles = touch_ends(jax.random.randint(part_splits[4], (QBLK, MB), 0, KT), jax.random.fold_in(part_splits[4], 1), 0, KT - 1).astype(jnp.int32)
    return dict(bank=bank, queries=queries, keys=keys, labels=labels, mask_tiles=mask_tiles)


TAU = 0.12
NEG = -1e+30
EPS = 1e-06

def masked_scores(rows_q, rows_k, mask_rows, first):
    s = jnp.dot(rows_q, rows_k.T, preferred_element_type=jnp.float32) / TAU
    nq, nk = s.shape
    ids = (first + jnp.arange(nk // TILE, dtype=jnp.int32)).astype(jnp.int32)
    hit = jnp.any(mask_rows[:, :, None] == ids[None, None, :], axis=1)
    live = jnp.broadcast_to(jnp.logical_not(hit)[:, None, :, None], (nq // TILE, TILE, nk // TILE, TILE)).reshape(nq, nk)
    return (jnp.where(live, s, NEG), live)

def reference(bank, queries, keys, labels, mask_tiles):
    block = math.gcd(BANK, 16384)
    count = BANK // block
    eta = 0.25 * BANK / QUERIES
    key_rows = keys[labels]
    pos = lax.optimization_barrier(jnp.sum(queries.astype(jnp.float32) * key_rows.astype(jnp.float32), axis=1)) / TAU
    groups = bank.reshape(count, block, D)
    starts = (jnp.arange(count, dtype=jnp.int32) * (block // TILE)).astype(jnp.int32)

    def stats(carry, item):
        top, total = carry
        rows, first = item
        s, live = masked_scores(queries, rows, mask_tiles, first)
        cmax = lax.optimization_barrier(jnp.max(s, axis=1))
        csum = lax.optimization_barrier(jnp.sum(jnp.where(live, jnp.exp(s - cmax[:, None]), 0.0), axis=1))
        high = jnp.maximum(top, cmax)
        return ((high, total * jnp.exp(top - high) + csum * jnp.exp(cmax - high)), None)
    init = (jnp.full((QUERIES,), NEG, jnp.float32), jnp.zeros((QUERIES,), jnp.float32))
    (top, total), unused = lax.scan(stats, init, (groups, starts))
    high = jnp.maximum(top, pos)
    lse = high + jnp.log(total * jnp.exp(top - high) + jnp.exp(pos - high))
    loss = lse - pos

    def grads(neg, item):
        rows, first = item
        s, live = masked_scores(queries, rows, mask_tiles, first)
        probs = jnp.exp(s - lse[:, None]).astype(jnp.bfloat16)
        neg = neg + jnp.dot(probs, rows, preferred_element_type=jnp.float32)
        pull = jnp.dot(probs.T, queries, preferred_element_type=jnp.float32)
        fresh = rows.astype(jnp.float32) + eta * pull
        fresh = fresh * lax.rsqrt(lax.optimization_barrier(jnp.mean(fresh * fresh, axis=1, keepdims=True)) + EPS)
        return (neg, fresh.astype(jnp.bfloat16))
    neg, fresh = lax.scan(grads, jnp.zeros((QUERIES, D), jnp.float32), (groups, starts))
    query_grad = (neg + (jnp.exp(pos - lse) - 1.0)[:, None] * key_rows.astype(jnp.float32)) / TAU
    return (fresh.reshape(BANK, D), query_grad, loss)
```

```python
import functools
import math

import jax
import jax.numpy as jnp
from jax import lax
from jax.experimental import pallas as pl
from jax.experimental.pallas import tpu as pltpu
from jax.sharding import PartitionSpec as P

TILE = 128


TAU = 0.12
NEG = -1e30
FLOOR = -1e29
EPS = 1e-06
LOG2E = math.log2(math.e)
LN2 = math.log(2.0)
SCALE2 = LOG2E / TAU
QCH = 256
BCH = 256
MESH = pl.DeviceIdType.MESH


def masked_scores(rows_q, rows_k, mask_rows, first):
    s = jnp.einsum("qd,kd->qk", rows_q, rows_k, preferred_element_type=jnp.float32) / TAU
    nq, nk = s.shape
    ids = first + jnp.arange(nk // TILE, dtype=jnp.int32)
    hit = jnp.any(mask_rows[:, :, None] == ids[None, None, :], axis=1)
    live = jnp.broadcast_to(
        jnp.logical_not(hit)[:, None, :, None], (nq // TILE, TILE, nk // TILE, TILE)
    ).reshape(nq, nk)
    return (jnp.where(live, s, NEG), live)


def general(bank, queries, keys, labels, mask_tiles):
    qdev = queries.shape[0]
    bdev = bank.shape[0]
    total_bank = bdev * lax.axis_size("bank")
    total_query = qdev * lax.axis_size("batch")
    eta = 0.25 * total_bank / total_query
    mine = lax.axis_index("batch")
    first = lax.axis_index("bank") * (bdev // TILE)
    all_keys = lax.all_gather(keys, "batch", axis=0, tiled=True)
    key_rows = jnp.take(all_keys, labels, axis=0)
    pos = jnp.sum(queries.astype(jnp.float32) * key_rows.astype(jnp.float32), axis=1) / TAU
    own_mask = lax.dynamic_slice_in_dim(mask_tiles, mine * (qdev // TILE), qdev // TILE, 0)
    scores, live = masked_scores(queries, bank, own_mask, first)
    top = lax.pmax(jnp.max(scores, axis=1), "bank")
    part_sum = jnp.sum(jnp.where(live, jnp.exp(scores - top[:, None]), 0.0), axis=1)
    total = lax.psum(part_sum, "bank")
    high = jnp.maximum(top, pos)
    lse = high + jnp.log(total * jnp.exp(top - high) + jnp.exp(pos - high))
    loss = lse - pos
    probs = jnp.exp(scores - lse[:, None]).astype(jnp.bfloat16)
    neg_local = jnp.dot(probs, bank, preferred_element_type=jnp.float32)
    own_pull = jnp.einsum("qk,qd->kd", probs, queries, preferred_element_type=jnp.float32)
    neg = lax.psum(neg_local, "bank")
    query_grad = (neg + (jnp.exp(pos - lse) - 1.0)[:, None] * key_rows.astype(jnp.float32)) / TAU
    pull = lax.psum(own_pull.astype(jnp.bfloat16), "batch").astype(jnp.float32)
    fresh = bank.astype(jnp.float32) + eta * pull
    fresh = fresh * lax.rsqrt(jnp.mean(fresh * fresh, axis=1, keepdims=True) + EPS)
    return (fresh.astype(jnp.bfloat16), query_grad, loss)


def column(row):
    return jnp.transpose(jnp.broadcast_to(row, (TILE, TILE)))


def wide_column(row, width):
    return jnp.concatenate([column(row)] * (width // TILE), axis=1)


def step_kernel(
    n, eta, mask_hbm, bank_hbm, q_hbm, keys_hbm, labels_hbm,
    new_hbm, grad_hbm, loss_ref,
    mask_ref, bank_ref, q_ref, keys_ref, labels_ref,
    s_scr, p_scr, bankt_scr, bias_scr, keys_scr, key_t_scr, stats_scr, pos_scr, qs_scr,
    stage_scr, square_scr, mirror_scr, grad_scr, pull_scr, pull_in_scr, new_scr,
    in_sems, keys_sems, stats_send, stats_recv, pos_send, pos_recv, square_send, square_recv,
    mirror_send, mirror_recv, grad_send, grad_recv, pull_send, pull_recv, out_sems, grad_sems,
):
    me = lax.axis_index("bank")
    mine = lax.axis_index("batch")
    other = 1 - mine
    bdev, width = bank_ref.shape
    qdev = q_ref.shape[0]
    tiles = bdev // TILE
    chunks = qdev // QCH
    parts = bdev // BCH
    listed = mask_ref.shape[1]
    first = me * tiles
    x = lax.rem(me, 2)
    zl = lax.rem(me // 2, 2)
    zh = me // 4
    quarter = zl * 2 + x

    pieces = 4
    piece = bdev // pieces
    mask_load = pltpu.make_async_copy(mask_hbm, mask_ref, in_sems.at[0])
    q_load = pltpu.make_async_copy(q_hbm, q_ref, in_sems.at[1])
    bank_loads = [
        pltpu.make_async_copy(bank_hbm.at[i * piece:(i + 1) * piece, :], bank_ref.at[i * piece:(i + 1) * piece, :], in_sems.at[4 + i])
        for i in range(pieces)]
    labels_load = pltpu.make_async_copy(labels_hbm, labels_ref, in_sems.at[2])
    keys_load = pltpu.make_async_copy(keys_hbm, keys_ref, in_sems.at[3])
    for load in [mask_load, q_load] + bank_loads + [labels_load, keys_load]:
        load.start()

    barrier = pltpu.get_barrier_semaphore()
    for d in range(1, n):
        pl.semaphore_signal(barrier, inc=1, device_id={"bank": lax.rem(me + d, n)}, device_id_type=MESH)
    pl.semaphore_signal(barrier, inc=1, device_id={"batch": other}, device_id_type=MESH)

    def peer(m):
        low = (1 - zl if m & 2 else zl) * 2 + (1 - x if m & 1 else x)
        return low, (1 - zh if m & 4 else zh) * 4 + low

    def to_bank(m, src, dst, send, recv):
        return pltpu.make_async_remote_copy(
            src_ref=src, dst_ref=dst, send_sem=send, recv_sem=recv,
            device_id={"bank": peer(m)[1]}, device_id_type=MESH)

    def to_core(src, dst, send, recv):
        return pltpu.make_async_remote_copy(
            src_ref=src, dst_ref=dst, send_sem=send, recv_sem=recv,
            device_id={"batch": other}, device_id_type=MESH)

    keys_copy = to_core(keys_hbm, keys_scr, keys_sems.at[0], keys_sems.at[1])
    stats = [[to_bank(m, stats_scr.at[c, me], stats_scr.at[c, me], stats_send.at[c * n + m], stats_recv.at[c * n + m])
              for m in range(1, n)] for c in range(chunks)]
    poses = [to_bank(m, pos_scr.at[quarter], pos_scr.at[quarter], pos_send.at[m], pos_recv.at[m]) for m in range(1, 4)]
    squares = [[to_bank(m, stage_scr.at[c, peer(m)[0]], square_scr.at[c, m - 1], square_send.at[c * 4 + m], square_recv.at[c * 4 + m])
                for m in range(1, 4)] for c in range(chunks)]
    mirrors = [to_bank(4, mirror_scr.at[c, zh], mirror_scr.at[c, zh], mirror_send.at[c], mirror_recv.at[c]) for c in range(chunks)]

    def grad_rows(c):
        return grad_hbm.at[x, pl.ds(pl.multiple_of(c * QCH + zl * TILE, TILE), TILE), :]

    grads = [[to_bank(m, grad_scr.at[c], grad_rows(c), grad_send.at[c * 4 + m], grad_recv.at[c * 4 + m])
              for m in range(1, 4)] for c in range(chunks)]
    own_grads = [pltpu.make_async_copy(grad_scr.at[c], grad_rows(c), grad_sems.at[c]) for c in range(chunks)]
    pulls = [to_core(pull_scr.at[k * BCH:(k + 1) * BCH, :], pull_in_scr.at[k * BCH:(k + 1) * BCH, :], pull_send.at[k], pull_recv.at[k])
             for k in range(parts)]
    outs = [pltpu.make_async_copy(new_scr.at[k * BCH:(k + 1) * BCH, :], new_hbm.at[k * BCH:(k + 1) * BCH, :], out_sems.at[k])
            for k in range(parts)]

    mask_load.wait()
    ids = first + lax.broadcasted_iota(jnp.int32, (tiles, listed), 0)
    for b in range(qdev // TILE):
        hit = jnp.where(ids == mask_ref[pl.ds(mine * (qdev // TILE) + b, 1), :], 1.0, 0.0)
        bias_scr[b] = jnp.broadcast_to(jnp.max(hit, axis=1, keepdims=True), (tiles, TILE)) * NEG

    def compute(c):
        cols = slice(c * QCH, (c + 1) * QCH)
        bias = [jnp.concatenate([bias_scr[c * (QCH // TILE) + u, t:t + 1, :] for u in range(QCH // TILE)], axis=1) for t in range(tiles)]
        qc = q_ref[cols, :]
        top8 = jnp.full((8, QCH), FLOOR / SCALE2, jnp.float32)
        for k in range(parts):
            if c == 0 and k * BCH % piece == 0:
                bank_loads[k * BCH // piece].wait()
            s = lax.dot_general(bank_ref[k * BCH:(k + 1) * BCH, :], qc, (((1,), (1,)), ((), ())),
                                preferred_element_type=jnp.float32)
            s_scr[c % 2, k * BCH:(k + 1) * BCH, :] = s
            for t in range(BCH // TILE):
                part = s[t * TILE:(t + 1) * TILE, :].reshape(TILE // 8, 8, QCH)
                top8 = jnp.maximum(top8, jnp.max(part, axis=0) + bias[k * (BCH // TILE) + t])
            if c == 0:
                bankt_scr[:, k * BCH:(k + 1) * BCH] = jnp.transpose(bank_ref[k * BCH:(k + 1) * BCH, :])
        top = jnp.max(top8, axis=0, keepdims=True) * SCALE2
        sum8 = jnp.zeros((8, QCH), jnp.float32)
        for t in range(tiles):
            rows = slice(t * TILE, (t + 1) * TILE)
            p = jnp.exp2(s_scr[c % 2, rows, :] * SCALE2 - (top - bias[t]))
            sum8 = sum8 + jnp.sum(p.reshape(TILE // 8, 8, QCH), axis=0)
            p_scr[rows, cols] = p.astype(jnp.bfloat16)
        total = jnp.sum(sum8, axis=0, keepdims=True)
        for u in range(QCH // TILE):
            stats_scr[c, me, u:u + 1, :] = top[:, u * TILE:(u + 1) * TILE]
            stats_scr[c, me, 2 + u:3 + u, :] = total[:, u * TILE:(u + 1) * TILE]
        if c == 0:
            pl.semaphore_wait(barrier, n)
            keys_copy.start()
        for copy in stats[c]:
            copy.start()
        neg = jnp.dot(bankt_scr[...], p_scr[:, cols], preferred_element_type=jnp.float32).astype(jnp.bfloat16)
        for u in range(2):
            for h in range(2):
                stage_scr[c, u * 2 + h] = neg[h * TILE:(h + 1) * TILE, u * TILE:(u + 1) * TILE]
        for m in (3, 2, 1):
            squares[c][m - 1].start()

    def pick_keys():
        labels_load.wait()
        keys_load.wait()
        keys_copy.wait()
        half = pl.ds(pl.multiple_of(x * TILE, TILE), TILE)
        row_ids = lax.broadcasted_iota(jnp.int32, (qdev, TILE), 0)
        row8 = lax.broadcasted_iota(jnp.int32, (8, TILE), 0)

        def picked(table, labels):
            hot = jnp.where(row_ids == labels, 1.0, 0.0).astype(jnp.bfloat16)
            return lax.dot_general(hot, table, (((0,), (0,)), ((), ())), preferred_element_type=jnp.float32)

        tile = jnp.zeros((8, TILE), jnp.float32)
        for c in range(chunks):
            labels = labels_ref[pl.ds(2 * c + zl, 1), :]
            rows = picked(keys_ref[:, half], labels - mine * qdev) + picked(keys_scr[:, half], labels - other * qdev)
            key_t = jnp.transpose(rows)
            key_t_scr[c] = key_t
            own = pl.ds(pl.multiple_of(c * QCH + zl * TILE, TILE), TILE)
            q_t = jnp.transpose(q_ref[own, half].astype(jnp.float32))
            pos = jnp.sum(key_t * q_t, axis=0, keepdims=True) * SCALE2
            tile = jnp.where(row8 == 2 * c + zl, pos, tile)
        pos_scr[quarter] = tile
        for copy in poses:
            copy.start()

    def own_row(c, b):
        return stats_scr[c, b, pl.ds(zl, 1), :]

    def combine(c):
        for m in range(1, 4):
            stats[c][m - 1].wait_recv()
            squares[c][m - 1].wait_recv()
        tops = [own_row(c, peer(m)[1]) for m in range(4)]
        both = jnp.maximum(jnp.maximum(tops[0], tops[1]), jnp.maximum(tops[2], tops[3]))
        total = stage_scr[c, quarter].astype(jnp.float32) * jnp.exp2(tops[0] - both)
        for m in range(1, 4):
            total = total + square_scr[c, m - 1].astype(jnp.float32) * jnp.exp2(tops[m] - both)
        mirror_scr[c, zh] = total.astype(jnp.bfloat16)
        mirrors[c].start()

    def settle(c, pos_all):
        for m in range(4, n):
            stats[c][m - 1].wait_recv()
        pos = pos_all[2 * c:2 * c + 2, :]
        high = pos
        for b in range(n):
            high = jnp.maximum(high, stats_scr[c, b, 0:2, :])
        total = jnp.exp2(pos - high)
        for b in range(n):
            total = total + stats_scr[c, b, 2:4, :] * jnp.exp2(stats_scr[c, b, 0:2, :] - high)
        lse = high + jnp.log(total) * LOG2E
        loss_ref[2 * c:2 * c + 2, :] = (lse - pos) * LN2
        alpha = jnp.exp2(stats_scr[c, me, 0:2, :] - lse)
        for u in range(2):
            rows = slice(c * QCH + u * TILE, c * QCH + (u + 1) * TILE)
            qs_scr[rows, :] = (q_ref[rows, :].astype(jnp.float32) * wide_column(alpha[u:u + 1, :], width)).astype(jnp.bfloat16)
        return jnp.where(zl == 0, lse[0:1, :], lse[1:2, :]), jnp.where(zl == 0, pos[0:1, :], pos[1:2, :])

    def finalize(c, lse, pos):
        mirrors[c].wait_recv()
        neg = None
        for side in range(2):
            top = own_row(c, side * 4)
            for b in range(1, 4):
                top = jnp.maximum(top, own_row(c, side * 4 + b))
            term = mirror_scr[c, side].astype(jnp.float32) * jnp.exp2(top - lse)
            neg = term if neg is None else neg + term
        grad = (neg + (jnp.exp2(pos - lse) - 1.0) * key_t_scr[c]) * (1.0 / TAU)
        grad_scr[c] = jnp.transpose(grad).astype(jnp.bfloat16)
        for m in (3, 2, 1):
            grads[c][m - 1].start()
        own_grads[c].start()

    def pull(k):
        rows = slice(k * BCH, (k + 1) * BCH)
        pull_scr[rows, :] = jnp.dot(p_scr[rows, :], qs_scr[...], preferred_element_type=jnp.float32).astype(jnp.bfloat16)
        pulls[k].start()

    def renew(k):
        rows = slice(k * BCH, (k + 1) * BCH)
        pulls[k].wait()
        both = pull_scr[rows, :].astype(jnp.float32) + pull_in_scr[rows, :].astype(jnp.float32)
        fresh = bank_ref[rows, :].astype(jnp.float32) + eta * both
        fresh = fresh * lax.rsqrt(jnp.mean(fresh * fresh, axis=1, keepdims=True) + EPS)
        new_scr[rows, :] = fresh.astype(jnp.bfloat16)
        outs[k].start()

    q_load.wait()
    for c in range(chunks):
        compute(c)
    pick_keys()
    for c in range(chunks):
        combine(c)
    for copy in poses:
        copy.wait_recv()
    pos_all = pos_scr[0]
    for j in range(1, 4):
        pos_all = pos_all + pos_scr[j]
    settled = [settle(c, pos_all) for c in range(chunks)]
    finalize(0, *settled[0])
    for k in range(parts // 2):
        pull(k)
    finalize(1, *settled[1])
    for k in range(parts // 2, parts):
        pull(k)
    finalize(2, *settled[2])
    for k in range(parts // 2):
        renew(k)
    finalize(3, *settled[3])
    for k in range(parts // 2, parts):
        renew(k)

    for c in range(chunks):
        for m in range(1, 4):
            grads[c][m - 1].wait_recv()
        own_grads[c].wait()
    for k in range(parts):
        outs[k].wait()
    for c in range(chunks):
        for copy in stats[c] + squares[c] + grads[c] + [mirrors[c]]:
            copy.wait_send()
    for copy in poses:
        copy.wait_send()


def fused(bank, queries, keys, labels, mask_tiles):
    n = lax.axis_size("bank")
    qdev, width = queries.shape
    bdev = bank.shape[0]
    chunks = qdev // QCH
    eta = 0.25 * (bdev * n) / (qdev * lax.axis_size("batch"))
    vmem = pl.BlockSpec(memory_space=pltpu.VMEM)
    hbm = pl.BlockSpec(memory_space=pltpu.HBM)
    dma = pltpu.SemaphoreType.DMA
    new_bank, grad, loss = pl.pallas_call(
        functools.partial(step_kernel, n, eta),
        out_shape=(
            jax.ShapeDtypeStruct((bdev, width), jnp.bfloat16),
            jax.ShapeDtypeStruct((2, qdev, TILE), jnp.bfloat16),
            jax.ShapeDtypeStruct((n, TILE), jnp.float32),
        ),
        in_specs=[hbm] * 5,
        out_specs=(hbm, hbm, vmem),
        scratch_shapes=[
            pltpu.VMEM(mask_tiles.shape, jnp.int32),
            pltpu.VMEM((bdev, width), jnp.bfloat16),
            pltpu.VMEM((qdev, width), jnp.bfloat16),
            pltpu.VMEM((qdev, width), jnp.bfloat16),
            pltpu.VMEM((n, TILE), jnp.int32),
            pltpu.VMEM((2, bdev, QCH), jnp.float32),
            pltpu.VMEM((bdev, qdev), jnp.bfloat16),
            pltpu.VMEM((width, bdev), jnp.bfloat16),
            pltpu.VMEM((n, bdev // TILE, TILE), jnp.float32),
            pltpu.VMEM((qdev, width), jnp.bfloat16),
            pltpu.VMEM((chunks, TILE, TILE), jnp.float32),
            pltpu.VMEM((chunks, n, 8, TILE), jnp.float32),
            pltpu.VMEM((4, 8, TILE), jnp.float32),
            pltpu.VMEM((qdev, width), jnp.bfloat16),
            pltpu.VMEM((chunks, 4, TILE, TILE), jnp.bfloat16),
            pltpu.VMEM((chunks, 3, TILE, TILE), jnp.bfloat16),
            pltpu.VMEM((chunks, 2, TILE, TILE), jnp.bfloat16),
            pltpu.VMEM((chunks, TILE, TILE), jnp.bfloat16),
            pltpu.VMEM((bdev, width), jnp.bfloat16),
            pltpu.VMEM((bdev, width), jnp.bfloat16),
            pltpu.VMEM((bdev, width), jnp.bfloat16),
            dma((8,)),
            dma((2,)),
            dma((chunks * n,)), dma((chunks * n,)),
            dma((4,)), dma((4,)),
            dma((chunks * 4,)), dma((chunks * 4,)),
            dma((chunks,)), dma((chunks,)),
            dma((chunks * 4,)), dma((chunks * 4,)),
            dma((bdev // BCH,)), dma((bdev // BCH,)),
            dma((bdev // BCH,)),
            dma((chunks,)),
        ],
        compiler_params=pltpu.CompilerParams(
            collective_id=0, has_side_effects=True, vmem_limit_bytes=60 * 1024 * 1024
        ),
    )(mask_tiles, bank, queries, keys, labels.reshape(n, TILE))
    new_bank, query_grad, loss = finish(new_bank, grad, loss)
    return (new_bank, query_grad, loss.reshape(qdev))


def finish_kernel(bank_in, grad_in, loss_in, bank_out, grad_out, loss_out):
    bank_out[...] = bank_in[...]
    grad_out[:, :TILE] = grad_in[0].astype(jnp.float32)
    grad_out[:, TILE:] = grad_in[1].astype(jnp.float32)
    loss_out[...] = loss_in[...]


def finish(new_bank, grad, loss):
    bdev, width = new_bank.shape
    qdev = grad.shape[1]
    steps = 2
    whole = pl.BlockSpec(loss.shape, lambda i: (0, 0))
    bank_spec = pl.BlockSpec((bdev // steps, width), lambda i: (i, 0))
    return pl.pallas_call(
        finish_kernel,
        grid=(steps,),
        out_shape=(
            jax.ShapeDtypeStruct((bdev, width), jnp.bfloat16),
            jax.ShapeDtypeStruct((qdev, width), jnp.float32),
            jax.ShapeDtypeStruct(loss.shape, jnp.float32),
        ),
        in_specs=[bank_spec, pl.BlockSpec((2, qdev // steps, TILE), lambda i: (0, i, 0)), whole],
        out_specs=(bank_spec, pl.BlockSpec((qdev // steps, width), lambda i: (i, 0)), whole),
    )(new_bank, grad, loss)


def on_device(bank, queries, keys, labels, mask_tiles):
    n = lax.axis_size("bank")
    fits = (
        n == 8
        and queries.shape == (n * TILE, 2 * TILE)
        and bank.shape[0] % BCH == 0
        and lax.axis_size("batch") == 2
    )
    return (fused if fits else general)(bank, queries, keys, labels, mask_tiles)


def solution(mesh):
    return jax.shard_map(
        on_device,
        mesh=mesh,
        in_specs=(
            P(("parts", "bank"), None),
            P(("parts", "batch"), None),
            P(("parts", "batch"), None),
            P(("parts", "batch")),
            P("parts", None),
        ),
        out_specs=(P(("parts", "bank"), None), P(("parts", "batch"), None), P(("parts", "batch"))),
        check_vma=False,
    )
```

```python
import functools
import math

import jax
import jax.numpy as jnp
from jax import lax
from jax.experimental import pallas as pl
from jax.experimental.pallas import tpu as pltpu
from jax.sharding import PartitionSpec as P

TILE = 128


TAU = 0.12
NEG = -1e30
FLOOR = -1e29
EPS = 1e-06
LOG2E = math.log2(math.e)
LN2 = math.log(2.0)
SCALE2 = LOG2E / TAU
QCH = 256
BCH = 256
MESH = pl.DeviceIdType.MESH


def masked_scores(rows_q, rows_k, mask_rows, first):
    s = jnp.einsum("qd,kd->qk", rows_q, rows_k, preferred_element_type=jnp.float32) / TAU
    nq, nk = s.shape
    ids = first + jnp.arange(nk // TILE, dtype=jnp.int32)
    hit = jnp.any(mask_rows[:, :, None] == ids[None, None, :], axis=1)
    live = jnp.broadcast_to(
        jnp.logical_not(hit)[:, None, :, None], (nq // TILE, TILE, nk // TILE, TILE)
    ).reshape(nq, nk)
    return (jnp.where(live, s, NEG), live)


def general(bank, queries, keys, labels, mask_tiles):
    qdev = queries.shape[0]
    bdev = bank.shape[0]
    total_bank = bdev * lax.axis_size("bank")
    total_query = qdev * lax.axis_size("batch")
    eta = 0.25 * total_bank / total_query
    mine = lax.axis_index("batch")
    first = lax.axis_index("bank") * (bdev // TILE)
    all_keys = lax.all_gather(keys, "batch", axis=0, tiled=True)
    key_rows = jnp.take(all_keys, labels, axis=0)
    pos = jnp.sum(queries.astype(jnp.float32) * key_rows.astype(jnp.float32), axis=1) / TAU
    own_mask = lax.dynamic_slice_in_dim(mask_tiles, mine * (qdev // TILE), qdev // TILE, 0)
    scores, live = masked_scores(queries, bank, own_mask, first)
    top = lax.pmax(jnp.max(scores, axis=1), "bank")
    part_sum = jnp.sum(jnp.where(live, jnp.exp(scores - top[:, None]), 0.0), axis=1)
    total = lax.psum(part_sum, "bank")
    high = jnp.maximum(top, pos)
    lse = high + jnp.log(total * jnp.exp(top - high) + jnp.exp(pos - high))
    loss = lse - pos
    probs = jnp.exp(scores - lse[:, None]).astype(jnp.bfloat16)
    neg_local = jnp.dot(probs, bank, preferred_element_type=jnp.float32)
    own_pull = jnp.einsum("qk,qd->kd", probs, queries, preferred_element_type=jnp.float32)
    neg = lax.psum(neg_local, "bank")
    query_grad = (neg + (jnp.exp(pos - lse) - 1.0)[:, None] * key_rows.astype(jnp.float32)) / TAU
    pull = lax.psum(own_pull.astype(jnp.bfloat16), "batch").astype(jnp.float32)
    fresh = bank.astype(jnp.float32) + eta * pull
    fresh = fresh * lax.rsqrt(jnp.mean(fresh * fresh, axis=1, keepdims=True) + EPS)
    return (fresh.astype(jnp.bfloat16), query_grad, loss)


def column(row):
    return jnp.transpose(jnp.broadcast_to(row, (TILE, TILE)))


def wide_column(row, width):
    return jnp.concatenate([column(row)] * (width // TILE), axis=1)


def step_kernel(
    n, eta, mask_hbm, bank_hbm, q_hbm, keys_hbm, labels_hbm,
    new_ref, grad_ref, loss_ref,
    mask_ref, bank_ref, q_ref, keys_ref, labels_ref,
    s_scr, p_scr, bankt_scr, bias_scr, keys_scr, key_t_scr, stats_scr, pos_scr, qs_scr,
    stage_scr, square_scr, mirror_scr, pull_scr, pull_in_scr,
    in_sems, keys_sems, send_sems, pos_recv, stats_recv, square_recv, mirror_recv, grad_recv, pull_recv,
):
    me = lax.axis_index("bank")
    mine = lax.axis_index("batch")
    other = 1 - mine
    bdev, width = bank_ref.shape
    qdev = q_ref.shape[0]
    tiles = bdev // TILE
    chunks = qdev // QCH
    parts = bdev // BCH
    listed = mask_ref.shape[1]
    first = me * tiles
    x = lax.rem(me, 2)
    zl = lax.rem(me // 2, 2)
    zh = me // 4
    quarter = zl * 2 + x

    pieces = 4
    piece = bdev // pieces
    mask_load = pltpu.make_async_copy(mask_hbm, mask_ref, in_sems.at[0])
    q_load = pltpu.make_async_copy(q_hbm, q_ref, in_sems.at[1])
    bank_loads = [
        pltpu.make_async_copy(bank_hbm.at[i * piece:(i + 1) * piece, :], bank_ref.at[i * piece:(i + 1) * piece, :], in_sems.at[4 + i])
        for i in range(pieces)]
    labels_load = pltpu.make_async_copy(labels_hbm, labels_ref, in_sems.at[2])
    keys_load = pltpu.make_async_copy(keys_hbm, keys_ref, in_sems.at[3])
    for load in [mask_load, q_load] + bank_loads + [labels_load, keys_load]:
        load.start()

    barrier = pltpu.get_barrier_semaphore()
    for d in range(1, n):
        pl.semaphore_signal(barrier, inc=1, device_id={"bank": lax.rem(me + d, n)}, device_id_type=MESH)
    pl.semaphore_signal(barrier, inc=1, device_id={"batch": other}, device_id_type=MESH)

    def peer(m):
        low = (1 - zl if m & 2 else zl) * 2 + (1 - x if m & 1 else x)
        return low, (1 - zh if m & 4 else zh) * 4 + low

    def to_bank(m, src, dst, send, recv):
        return pltpu.make_async_remote_copy(
            src_ref=src, dst_ref=dst, send_sem=send, recv_sem=recv,
            device_id={"bank": peer(m)[1]}, device_id_type=MESH)

    def to_core(src, dst, send, recv):
        return pltpu.make_async_remote_copy(
            src_ref=src, dst_ref=dst, send_sem=send, recv_sem=recv,
            device_id={"batch": other}, device_id_type=MESH)

    keys_copy = to_core(keys_hbm, keys_scr, keys_sems.at[0], keys_sems.at[1])
    def drain(ref, sem):
        pltpu.make_async_copy(ref, ref, sem).wait()

    stats_send, pos_send, square_send, mirror_send, grad_send, pull_send = [send_sems.at[i] for i in range(6)]
    stats = [[to_bank(m, stats_scr.at[c, me], stats_scr.at[c, me], stats_send, stats_recv.at[c])
              for m in range(1, n)] for c in range(chunks)]
    poses = [to_bank(m, pos_scr.at[quarter], pos_scr.at[quarter], pos_send, pos_recv.at[0]) for m in range(1, 4)]
    squares = [[to_bank(m, stage_scr.at[c, peer(m)[0]], square_scr.at[c, m - 1], square_send, square_recv.at[c])
                for m in range(1, 4)] for c in range(chunks)]
    mirrors = [to_bank(4, mirror_scr.at[c, zh], mirror_scr.at[c, zh], mirror_send, mirror_recv.at[c]) for c in range(chunks)]

    def grad_rows(c):
        return grad_ref.at[x, pl.ds(pl.multiple_of(c * QCH + zl * TILE, TILE), TILE), :]

    grads = [[to_bank(m, grad_rows(c), grad_rows(c), grad_send, grad_recv.at[0])
              for m in range(1, 4)] for c in range(chunks)]
    sends = 4
    span = bdev // sends
    pulls = [to_core(pull_scr.at[k * span:(k + 1) * span, :], pull_in_scr.at[k * span:(k + 1) * span, :], pull_send, pull_recv.at[k])
             for k in range(sends)]

    mask_load.wait()
    ids = first + lax.broadcasted_iota(jnp.int32, (tiles, listed), 0)
    for b in range(qdev // TILE):
        hit = jnp.where(ids == mask_ref[pl.ds(mine * (qdev // TILE) + b, 1), :], 1.0, 0.0)
        bias_scr[b] = jnp.broadcast_to(jnp.max(hit, axis=1, keepdims=True), (tiles, TILE)) * NEG

    def compute(c):
        cols = slice(c * QCH, (c + 1) * QCH)
        bias = [jnp.concatenate([bias_scr[c * (QCH // TILE) + u, t:t + 1, :] for u in range(QCH // TILE)], axis=1) for t in range(tiles)]
        qc = q_ref[cols, :]
        top8 = jnp.full((8, QCH), FLOOR / SCALE2, jnp.float32)
        for k in range(parts):
            if c == 0 and k * BCH % piece == 0:
                bank_loads[k * BCH // piece].wait()
            s = lax.dot_general(bank_ref[k * BCH:(k + 1) * BCH, :], qc, (((1,), (1,)), ((), ())),
                                preferred_element_type=jnp.float32)
            s_scr[c % 2, k * BCH:(k + 1) * BCH, :] = s
            for t in range(BCH // TILE):
                part = s[t * TILE:(t + 1) * TILE, :].reshape(TILE // 8, 8, QCH)
                top8 = jnp.maximum(top8, jnp.max(part, axis=0) + bias[k * (BCH // TILE) + t])
            if c == 0:
                bankt_scr[:, k * BCH:(k + 1) * BCH] = jnp.transpose(bank_ref[k * BCH:(k + 1) * BCH, :])
        top = jnp.max(top8, axis=0, keepdims=True) * SCALE2
        sum8 = jnp.zeros((8, QCH), jnp.float32)
        for t in range(tiles):
            rows = slice(t * TILE, (t + 1) * TILE)
            p = jnp.exp2(s_scr[c % 2, rows, :] * SCALE2 - (top - bias[t]))
            sum8 = sum8 + jnp.sum(p.reshape(TILE // 8, 8, QCH), axis=0)
            p_scr[rows, cols] = p.astype(jnp.bfloat16)
        total = jnp.sum(sum8, axis=0, keepdims=True)
        for u in range(QCH // TILE):
            stats_scr[c, me, u:u + 1, :] = top[:, u * TILE:(u + 1) * TILE]
            stats_scr[c, me, 2 + u:3 + u, :] = total[:, u * TILE:(u + 1) * TILE]
        if c == 0:
            pl.semaphore_wait(barrier, n)
            keys_copy.start()
        for copy in stats[c]:
            copy.start()
        neg = jnp.dot(bankt_scr[...], p_scr[:, cols], preferred_element_type=jnp.float32).astype(jnp.bfloat16)
        for u in range(2):
            for h in range(2):
                stage_scr[c, u * 2 + h] = neg[h * TILE:(h + 1) * TILE, u * TILE:(u + 1) * TILE]
        for m in (3, 2, 1):
            squares[c][m - 1].start()

    def pick_keys():
        labels_load.wait()
        keys_load.wait()
        keys_copy.wait()
        half = pl.ds(pl.multiple_of(x * TILE, TILE), TILE)
        row_ids = lax.broadcasted_iota(jnp.int32, (qdev, TILE), 0)
        row8 = lax.broadcasted_iota(jnp.int32, (8, TILE), 0)

        def picked(table, labels):
            hot = jnp.where(row_ids == labels, 1.0, 0.0).astype(jnp.bfloat16)
            return lax.dot_general(hot, table, (((0,), (0,)), ((), ())), preferred_element_type=jnp.float32)

        tile = jnp.zeros((8, TILE), jnp.float32)
        for c in range(chunks):
            labels = labels_ref[pl.ds(2 * c + zl, 1), :]
            rows = picked(keys_ref[:, half], labels - mine * qdev) + picked(keys_scr[:, half], labels - other * qdev)
            key_t = jnp.transpose(rows)
            key_t_scr[c] = key_t
            own = pl.ds(pl.multiple_of(c * QCH + zl * TILE, TILE), TILE)
            q_t = jnp.transpose(q_ref[own, half].astype(jnp.float32))
            pos = jnp.sum(key_t * q_t, axis=0, keepdims=True) * SCALE2
            tile = jnp.where(row8 == 2 * c + zl, pos, tile)
        pos_scr[quarter] = tile
        for copy in poses:
            copy.start()

    def own_row(c, b):
        return stats_scr[c, b, pl.ds(zl, 1), :]

    def combine(c):
        if c < 3:
            drain(stats_scr.at[c, 0:n - 1], stats_recv.at[c])
        drain(square_scr.at[c], square_recv.at[c])
        tops = [own_row(c, peer(m)[1]) for m in range(4)]
        both = jnp.maximum(jnp.maximum(tops[0], tops[1]), jnp.maximum(tops[2], tops[3]))
        total = stage_scr[c, quarter].astype(jnp.float32) * jnp.exp2(tops[0] - both)
        for m in range(1, 4):
            total = total + square_scr[c, m - 1].astype(jnp.float32) * jnp.exp2(tops[m] - both)
        mirror_scr[c, zh] = total.astype(jnp.bfloat16)
        mirrors[c].start()

    def settle(c, pos_all):
        pos = pos_all[2 * c:2 * c + 2, :]
        high = pos
        for b in range(n):
            high = jnp.maximum(high, stats_scr[c, b, 0:2, :])
        total = jnp.exp2(pos - high)
        for b in range(n):
            total = total + stats_scr[c, b, 2:4, :] * jnp.exp2(stats_scr[c, b, 0:2, :] - high)
        lse = high + jnp.log(total) * LOG2E
        loss_ref[2 * c:2 * c + 2, :] = (lse - pos) * LN2
        alpha = jnp.exp2(stats_scr[c, me, 0:2, :] - lse)
        for u in range(2):
            rows = slice(c * QCH + u * TILE, c * QCH + (u + 1) * TILE)
            qs_scr[rows, :] = (q_ref[rows, :].astype(jnp.float32) * wide_column(alpha[u:u + 1, :], width)).astype(jnp.bfloat16)
        return jnp.where(zl == 0, lse[0:1, :], lse[1:2, :]), jnp.where(zl == 0, pos[0:1, :], pos[1:2, :])

    def finalize(c, lse, pos):
        mirrors[c].wait_recv()
        neg = None
        for side in range(2):
            top = own_row(c, side * 4)
            for b in range(1, 4):
                top = jnp.maximum(top, own_row(c, side * 4 + b))
            term = mirror_scr[c, side].astype(jnp.float32) * jnp.exp2(top - lse)
            neg = term if neg is None else neg + term
        grad = (neg + (jnp.exp2(pos - lse) - 1.0) * key_t_scr[c]) * (1.0 / TAU)
        grad_rows(c)[...] = jnp.transpose(grad).astype(jnp.bfloat16)
        for m in (3, 2, 1):
            grads[c][m - 1].start()

    def pull(k):
        rows = slice(k * span, (k + 1) * span)
        pull_scr[rows, :] = jnp.dot(p_scr[rows, :], qs_scr[...], preferred_element_type=jnp.float32).astype(jnp.bfloat16)
        pulls[k].start()

    def renew(k):
        pulls[k].wait_recv()
        for i in range(span // BCH):
            rows = slice(k * span + i * BCH, k * span + (i + 1) * BCH)
            both = pull_scr[rows, :].astype(jnp.float32) + pull_in_scr[rows, :].astype(jnp.float32)
            fresh = bank_ref[rows, :].astype(jnp.float32) + eta * both
            fresh = fresh * lax.rsqrt(jnp.mean(fresh * fresh, axis=1, keepdims=True) + EPS)
            new_ref[rows, :] = fresh.astype(jnp.bfloat16)

    q_load.wait()
    for c in range(chunks):
        compute(c)
    pick_keys()
    combine(0)
    combine(1)
    drain(pos_scr.at[0:3], pos_recv.at[0])
    pos_all = pos_scr[0]
    for j in range(1, 4):
        pos_all = pos_all + pos_scr[j]
    settled = [settle(c, pos_all) for c in range(2)]
    combine(2)
    drain(stats_scr.at[3, 0:n - 1], stats_recv.at[3])
    settled += [settle(c, pos_all) for c in range(2, 4)]
    pull(0)
    pull(1)
    combine(3)
    finalize(0, *settled[0])
    pull(2)
    pull(3)
    finalize(1, *settled[1])
    renew(0)
    renew(1)
    finalize(2, *settled[2])
    renew(2)
    finalize(3, *settled[3])
    renew(3)

    drain(grad_ref.at[:, 0:qdev * 3 // 4, :], grad_recv.at[0])
    drain(stats_scr.at[:, 0:n - 1], stats_send)
    drain(pos_scr.at[0:3], pos_send)
    drain(square_scr, square_send)
    drain(mirror_scr.at[:, 0], mirror_send)
    drain(grad_ref.at[:, 0:qdev * 3 // 4, :], grad_send)
    drain(pull_scr, pull_send)


def fused(bank, queries, keys, labels, mask_tiles):
    n = lax.axis_size("bank")
    qdev, width = queries.shape
    bdev = bank.shape[0]
    chunks = qdev // QCH
    eta = 0.25 * (bdev * n) / (qdev * lax.axis_size("batch"))
    vmem = pl.BlockSpec(memory_space=pltpu.VMEM)
    hbm = pl.BlockSpec(memory_space=pltpu.HBM)
    dma = pltpu.SemaphoreType.DMA
    new_bank, grad, loss = pl.pallas_call(
        functools.partial(step_kernel, n, eta),
        out_shape=(
            pltpu.VMEM((bdev, width), jnp.bfloat16),
            pltpu.VMEM((2, qdev, TILE), jnp.bfloat16),
            pltpu.VMEM((n, TILE), jnp.float32),
        ),
        in_specs=[hbm] * 5,
        out_specs=(vmem, vmem, vmem),
        scratch_shapes=[
            pltpu.VMEM(mask_tiles.shape, jnp.int32),
            pltpu.VMEM((bdev, width), jnp.bfloat16),
            pltpu.VMEM((qdev, width), jnp.bfloat16),
            pltpu.VMEM((qdev, width), jnp.bfloat16),
            pltpu.VMEM((n, TILE), jnp.int32),
            pltpu.VMEM((2, bdev, QCH), jnp.float32),
            pltpu.VMEM((bdev, qdev), jnp.bfloat16),
            pltpu.VMEM((width, bdev), jnp.bfloat16),
            pltpu.VMEM((n, bdev // TILE, TILE), jnp.float32),
            pltpu.VMEM((qdev, width), jnp.bfloat16),
            pltpu.VMEM((chunks, TILE, TILE), jnp.float32),
            pltpu.VMEM((chunks, n, 8, TILE), jnp.float32),
            pltpu.VMEM((4, 8, TILE), jnp.float32),
            pltpu.VMEM((qdev, width), jnp.bfloat16),
            pltpu.VMEM((chunks, 4, TILE, TILE), jnp.bfloat16),
            pltpu.VMEM((chunks, 3, TILE, TILE), jnp.bfloat16),
            pltpu.VMEM((chunks, 2, TILE, TILE), jnp.bfloat16),
            pltpu.VMEM((bdev, width), jnp.bfloat16),
            pltpu.VMEM((bdev, width), jnp.bfloat16),
            dma((8,)), dma((2,)), dma((6,)),
            dma((1,)), dma((chunks,)), dma((chunks,)), dma((chunks,)), dma((1,)), dma((4,)),
        ],
        compiler_params=pltpu.CompilerParams(
            collective_id=0, has_side_effects=True, vmem_limit_bytes=60 * 1024 * 1024
        ),
    )(mask_tiles, bank, queries, keys, labels.reshape(n, TILE))
    new_bank, query_grad, loss = finish(new_bank, grad, loss)
    return (new_bank, query_grad, loss.reshape(qdev))


def finish_kernel(bank_in, grad_in, loss_in, bank_out, grad_out, loss_out, out_scr, sems):
    qdev = grad_out.shape[0]
    steps = 4
    rows = qdev // steps
    copies = [pltpu.make_async_copy(bank_in, bank_out, sems.at[0]), pltpu.make_async_copy(loss_in, loss_out, sems.at[1])]
    for c in copies: c.start()
    for i in range(steps):
        r = slice(i * rows, (i + 1) * rows)
        out_scr[r, :TILE] = grad_in[0, r, :].astype(jnp.float32)
        out_scr[r, TILE:] = grad_in[1, r, :].astype(jnp.float32)
        copies.append(pltpu.make_async_copy(out_scr.at[r, :], grad_out.at[r, :], sems.at[2 + i]))
        copies[-1].start()
    for c in copies: c.wait()


def finish(new_bank, grad, loss):
    bdev, width = new_bank.shape
    qdev = grad.shape[1]
    hbm = pl.BlockSpec(memory_space=pltpu.HBM)
    return pl.pallas_call(
        finish_kernel,
        out_shape=(
            jax.ShapeDtypeStruct((bdev, width), jnp.bfloat16),
            jax.ShapeDtypeStruct((qdev, width), jnp.float32),
            jax.ShapeDtypeStruct(loss.shape, jnp.float32),
        ),
        in_specs=[pl.BlockSpec(memory_space=pltpu.VMEM)] * 3,
        out_specs=(hbm, hbm, hbm),
        scratch_shapes=[pltpu.VMEM((qdev, width), jnp.float32), pltpu.SemaphoreType.DMA((6,))],
        compiler_params=pltpu.CompilerParams(vmem_limit_bytes=16 * 1024 * 1024),
    )(new_bank, grad, loss)


def on_device(bank, queries, keys, labels, mask_tiles):
    n = lax.axis_size("bank")
    fits = (
        n == 8
        and queries.shape == (n * TILE, 2 * TILE)
        and bank.shape[0] % BCH == 0
        and lax.axis_size("batch") == 2
    )
    return (fused if fits else general)(bank, queries, keys, labels, mask_tiles)


def solution(mesh):
    return jax.shard_map(
        on_device,
        mesh=mesh,
        in_specs=(
            P(("parts", "bank"), None),
            P(("parts", "batch"), None),
            P(("parts", "batch"), None),
            P(("parts", "batch")),
            P("parts", None),
        ),
        out_specs=(P(("parts", "bank"), None), P(("parts", "batch"), None), P(("parts", "batch"))),
        check_vma=False,
    )
```

```python
import functools
import math

import jax
import jax.numpy as jnp
from jax import lax
from jax.experimental import pallas as pl
from jax.experimental.pallas import tpu as pltpu
from jax.sharding import PartitionSpec as P

TILE = 128


TAU = 0.12
NEG = -1e30
FLOOR = -1e29
EPS = 1e-06
LOG2E = math.log2(math.e)
LN2 = math.log(2.0)
SCALE2 = LOG2E / TAU
QCH = 256
BCH = 256
MESH = pl.DeviceIdType.MESH


def masked_scores(rows_q, rows_k, mask_rows, first):
    s = jnp.einsum("qd,kd->qk", rows_q, rows_k, preferred_element_type=jnp.float32) / TAU
    nq, nk = s.shape
    ids = first + jnp.arange(nk // TILE, dtype=jnp.int32)
    hit = jnp.any(mask_rows[:, :, None] == ids[None, None, :], axis=1)
    live = jnp.broadcast_to(
        jnp.logical_not(hit)[:, None, :, None], (nq // TILE, TILE, nk // TILE, TILE)
    ).reshape(nq, nk)
    return (jnp.where(live, s, NEG), live)


def general(bank, queries, keys, labels, mask_tiles):
    qdev = queries.shape[0]
    bdev = bank.shape[0]
    total_bank = bdev * lax.axis_size("bank")
    total_query = qdev * lax.axis_size("batch")
    eta = 0.25 * total_bank / total_query
    mine = lax.axis_index("batch")
    first = lax.axis_index("bank") * (bdev // TILE)
    all_keys = lax.all_gather(keys, "batch", axis=0, tiled=True)
    key_rows = jnp.take(all_keys, labels, axis=0)
    pos = jnp.sum(queries.astype(jnp.float32) * key_rows.astype(jnp.float32), axis=1) / TAU
    own_mask = lax.dynamic_slice_in_dim(mask_tiles, mine * (qdev // TILE), qdev // TILE, 0)
    scores, live = masked_scores(queries, bank, own_mask, first)
    top = lax.pmax(jnp.max(scores, axis=1), "bank")
    part_sum = jnp.sum(jnp.where(live, jnp.exp(scores - top[:, None]), 0.0), axis=1)
    total = lax.psum(part_sum, "bank")
    high = jnp.maximum(top, pos)
    lse = high + jnp.log(total * jnp.exp(top - high) + jnp.exp(pos - high))
    loss = lse - pos
    probs = jnp.exp(scores - lse[:, None]).astype(jnp.bfloat16)
    neg_local = jnp.dot(probs, bank, preferred_element_type=jnp.float32)
    own_pull = jnp.einsum("qk,qd->kd", probs, queries, preferred_element_type=jnp.float32)
    neg = lax.psum(neg_local, "bank")
    query_grad = (neg + (jnp.exp(pos - lse) - 1.0)[:, None] * key_rows.astype(jnp.float32)) / TAU
    pull = lax.psum(own_pull.astype(jnp.bfloat16), "batch").astype(jnp.float32)
    fresh = bank.astype(jnp.float32) + eta * pull
    fresh = fresh * lax.rsqrt(jnp.mean(fresh * fresh, axis=1, keepdims=True) + EPS)
    return (fresh.astype(jnp.bfloat16), query_grad, loss)


def column(row):
    return jnp.transpose(jnp.broadcast_to(row, (TILE, TILE)))


def wide_column(row, width):
    return jnp.concatenate([column(row)] * (width // TILE), axis=1)


def step_kernel(
    n, eta, mask_hbm, bank_hbm, q_hbm, keys_hbm, labels_hbm,
    new_ref, grad_ref, loss_ref,
    mask_ref, bank_ref, q_ref, keys_ref, labels_ref,
    s_scr, p_scr, bankt_scr, bias_scr, keys_scr, key_t_scr, stats_scr, level_scr, pos_scr, qs_scr,
    stage_scr, square_scr, mirror_scr, pull_scr, pull_in_scr,
    in_sems, keys_sems, send_sems, pos_recv, stats_recv, level_recv, square_recv, mirror_recv, grad_recv, pull_recv,
):
    me = lax.axis_index("bank")
    mine = lax.axis_index("batch")
    other = 1 - mine
    bdev, width = bank_ref.shape
    qdev = q_ref.shape[0]
    tiles = bdev // TILE
    chunks = qdev // QCH
    parts = bdev // BCH
    listed = mask_ref.shape[1]
    first = me * tiles
    x = lax.rem(me, 2)
    zl = lax.rem(me // 2, 2)
    zh = me // 4
    quarter = zl * 2 + x

    relayed = 1
    pieces = 4
    piece = bdev // pieces
    mask_load = pltpu.make_async_copy(mask_hbm, mask_ref, in_sems.at[0])
    q_load = pltpu.make_async_copy(q_hbm, q_ref, in_sems.at[1])
    bank_loads = [
        pltpu.make_async_copy(bank_hbm.at[i * piece:(i + 1) * piece, :], bank_ref.at[i * piece:(i + 1) * piece, :], in_sems.at[4 + i])
        for i in range(pieces)]
    labels_load = pltpu.make_async_copy(labels_hbm, labels_ref, in_sems.at[2])
    keys_load = pltpu.make_async_copy(keys_hbm, keys_ref, in_sems.at[3])
    for load in [mask_load, q_load] + bank_loads:
        load.start()

    barrier = pltpu.get_barrier_semaphore()
    for d in range(1, n):
        pl.semaphore_signal(barrier, inc=1, device_id={"bank": lax.rem(me + d, n)}, device_id_type=MESH)
    pl.semaphore_signal(barrier, inc=1, device_id={"batch": other}, device_id_type=MESH)

    def peer(m):
        low = (1 - zl if m & 2 else zl) * 2 + (1 - x if m & 1 else x)
        return low, (1 - zh if m & 4 else zh) * 4 + low

    def to_bank(m, src, dst, send, recv):
        return pltpu.make_async_remote_copy(
            src_ref=src, dst_ref=dst, send_sem=send, recv_sem=recv,
            device_id={"bank": peer(m)[1]}, device_id_type=MESH)

    def to_core(src, dst, send, recv):
        return pltpu.make_async_remote_copy(
            src_ref=src, dst_ref=dst, send_sem=send, recv_sem=recv,
            device_id={"batch": other}, device_id_type=MESH)

    keys_copy = to_core(keys_hbm, keys_scr, keys_sems.at[0], keys_sems.at[1])
    def drain(ref, sem):
        pltpu.make_async_copy(ref, ref, sem).wait()

    stats_send, level_send, pos_send, square_send, mirror_send, grad_send, pull_send = [send_sems.at[i] for i in range(7)]
    stats = [[to_bank(m, stats_scr.at[c, quarter], stats_scr.at[c, quarter], stats_send, stats_recv.at[c])
              for m in range(1, 4)] for c in range(chunks)]
    levels = [to_bank(4, level_scr.at[c, zh], level_scr.at[c, zh], level_send, level_recv.at[c]) for c in range(chunks)]
    poses = [to_bank(m, pos_scr.at[quarter], pos_scr.at[quarter], pos_send, pos_recv.at[0]) for m in range(1, 4)]
    squares = [[to_bank(m, stage_scr.at[c, peer(m)[0]], square_scr.at[c, m - 1], square_send, square_recv.at[c])
                for m in range(1, 4)] for c in range(chunks)]
    mirrors = [to_bank(4, mirror_scr.at[c, zh], mirror_scr.at[c, zh], mirror_send, mirror_recv.at[c]) for c in range(chunks)]

    def grad_rows(c):
        return grad_ref.at[x, pl.ds(pl.multiple_of(c * QCH + zl * TILE, TILE), TILE), :]

    grads = [[to_bank(m, grad_rows(c), grad_rows(c), grad_send, grad_recv.at[1 + c if m == 2 and c < relayed else 0])
              for m in range(1, 4)] for c in range(chunks)]

    def came_rows(c):
        return grad_ref.at[x, pl.ds(pl.multiple_of(c * QCH + (1 - zl) * TILE, TILE), TILE), :]

    relays = [to_bank(1, came_rows(c), came_rows(c), grad_send, grad_recv.at[0]) for c in range(relayed)]

    def relay(c):
        drain(came_rows(c), grad_recv.at[1 + c])
        relays[c].start()
    sends = 4
    span = bdev // sends
    pulls = [to_core(pull_scr.at[k * span:(k + 1) * span, :], pull_in_scr.at[k * span:(k + 1) * span, :], pull_send, pull_recv.at[k])
             for k in range(sends)]

    mask_load.wait()
    ids = first + lax.broadcasted_iota(jnp.int32, (tiles, listed), 0)
    for b in range(qdev // TILE):
        hit = jnp.where(ids == mask_ref[pl.ds(mine * (qdev // TILE) + b, 1), :], 1.0, 0.0)
        bias_scr[b] = jnp.broadcast_to(jnp.max(hit, axis=1, keepdims=True), (tiles, TILE)) * NEG

    def compute(c):
        cols = slice(c * QCH, (c + 1) * QCH)
        bias = [jnp.concatenate([bias_scr[c * (QCH // TILE) + u, t:t + 1, :] for u in range(QCH // TILE)], axis=1) for t in range(tiles)]
        qc = q_ref[cols, :]
        top8 = jnp.full((8, QCH), FLOOR / SCALE2, jnp.float32)
        for k in range(parts):
            if c == 0 and k * BCH % piece == 0:
                bank_loads[k * BCH // piece].wait()
            s = lax.dot_general(bank_ref[k * BCH:(k + 1) * BCH, :], qc, (((1,), (1,)), ((), ())),
                                preferred_element_type=jnp.float32)
            s_scr[c % 2, k * BCH:(k + 1) * BCH, :] = s
            for t in range(BCH // TILE):
                part = s[t * TILE:(t + 1) * TILE, :].reshape(TILE // 8, 8, QCH)
                top8 = jnp.maximum(top8, jnp.max(part, axis=0) + bias[k * (BCH // TILE) + t])
            if c == 0:
                bankt_scr[:, k * BCH:(k + 1) * BCH] = jnp.transpose(bank_ref[k * BCH:(k + 1) * BCH, :])
        top = jnp.max(top8, axis=0, keepdims=True) * SCALE2
        sum8 = jnp.zeros((8, QCH), jnp.float32)
        for t in range(tiles):
            rows = slice(t * TILE, (t + 1) * TILE)
            p = jnp.exp2(s_scr[c % 2, rows, :] * SCALE2 - (top - bias[t]))
            sum8 = sum8 + jnp.sum(p.reshape(TILE // 8, 8, QCH), axis=0)
            p_scr[rows, cols] = p.astype(jnp.bfloat16)
        total = jnp.sum(sum8, axis=0, keepdims=True)
        for u in range(QCH // TILE):
            stats_scr[c, quarter, u:u + 1, :] = top[:, u * TILE:(u + 1) * TILE]
            stats_scr[c, quarter, 2 + u:3 + u, :] = total[:, u * TILE:(u + 1) * TILE]
        if c == 0:
            labels_load.start()
            keys_load.start()
            pl.semaphore_wait(barrier, n)
        for copy in stats[c]:
            copy.start()
        neg = jnp.dot(bankt_scr[...], p_scr[:, cols], preferred_element_type=jnp.float32).astype(jnp.bfloat16)
        for u in range(2):
            for h in range(2):
                stage_scr[c, u * 2 + h] = neg[h * TILE:(h + 1) * TILE, u * TILE:(u + 1) * TILE]
        for m in (3, 2, 1):
            squares[c][m - 1].start()
        if c == 0:
            keys_copy.start()

    def pick_keys():
        labels_load.wait()
        keys_load.wait()
        keys_copy.wait()
        half = pl.ds(pl.multiple_of(x * TILE, TILE), TILE)
        row_ids = lax.broadcasted_iota(jnp.int32, (qdev, TILE), 0)
        row8 = lax.broadcasted_iota(jnp.int32, (8, TILE), 0)

        def picked(table, labels):
            hot = jnp.where(row_ids == labels, 1.0, 0.0).astype(jnp.bfloat16)
            return lax.dot_general(hot, table, (((0,), (0,)), ((), ())), preferred_element_type=jnp.float32)

        tile = jnp.zeros((8, TILE), jnp.float32)
        for c in range(chunks):
            labels = labels_ref[pl.ds(2 * c + zl, 1), :]
            rows = picked(keys_ref[:, half], labels - mine * qdev) + picked(keys_scr[:, half], labels - other * qdev)
            key_t = jnp.transpose(rows)
            key_t_scr[c] = key_t
            own = pl.ds(pl.multiple_of(c * QCH + zl * TILE, TILE), TILE)
            q_t = jnp.transpose(q_ref[own, half].astype(jnp.float32))
            pos = jnp.sum(key_t * q_t, axis=0, keepdims=True) * SCALE2
            tile = jnp.where(row8 == 2 * c + zl, pos, tile)
        pos_scr[quarter] = tile
        for copy in poses:
            copy.start()

    def level(c):
        drain(stats_scr.at[c, 0:3], stats_recv.at[c])
        top = stats_scr[c, 0, 0:2, :]
        for b in range(1, 4):
            top = jnp.maximum(top, stats_scr[c, b, 0:2, :])
        total = stats_scr[c, 0, 2:4, :] * jnp.exp2(stats_scr[c, 0, 0:2, :] - top)
        for b in range(1, 4):
            total = total + stats_scr[c, b, 2:4, :] * jnp.exp2(stats_scr[c, b, 0:2, :] - top)
        level_scr[c, zh, 0:2, :] = top
        level_scr[c, zh, 2:4, :] = total
        levels[c].start()

    def combine(c):
        drain(square_scr.at[c], square_recv.at[c])
        both = level_scr[c, zh, pl.ds(zl, 1), :]
        total = None
        for m in range(4):
            piece = stage_scr[c, quarter] if m == 0 else square_scr[c, m - 1]
            term = piece.astype(jnp.float32) * jnp.exp2(stats_scr[c, peer(m)[0], pl.ds(zl, 1), :] - both)
            total = term if m == 0 else total + term
        mirror_scr[c, zh] = total.astype(jnp.bfloat16)
        mirrors[c].start()

    def settle(c, pos_all):
        drain(level_scr.at[c, 0], level_recv.at[c])
        pos = pos_all[2 * c:2 * c + 2, :]
        tops = [level_scr[c, side, 0:2, :] for side in range(2)]
        high = jnp.maximum(pos, jnp.maximum(tops[0], tops[1]))
        total = jnp.exp2(pos - high)
        for side in range(2):
            total = total + level_scr[c, side, 2:4, :] * jnp.exp2(tops[side] - high)
        lse = high + jnp.log(total) * LOG2E
        loss_ref[2 * c:2 * c + 2, :] = (lse - pos) * LN2
        alpha = jnp.exp2(stats_scr[c, quarter, 0:2, :] - lse)
        for u in range(2):
            rows = slice(c * QCH + u * TILE, c * QCH + (u + 1) * TILE)
            qs_scr[rows, :] = (q_ref[rows, :].astype(jnp.float32) * wide_column(alpha[u:u + 1, :], width)).astype(jnp.bfloat16)
        return jnp.where(zl == 0, lse[0:1, :], lse[1:2, :]), jnp.where(zl == 0, pos[0:1, :], pos[1:2, :])

    def finalize(c, lse, pos):
        drain(mirror_scr.at[c, 0], mirror_recv.at[c])
        neg = None
        for side in range(2):
            term = mirror_scr[c, side].astype(jnp.float32) * jnp.exp2(level_scr[c, side, pl.ds(zl, 1), :] - lse)
            neg = term if neg is None else neg + term
        grad = (neg + (jnp.exp2(pos - lse) - 1.0) * key_t_scr[c]) * (1.0 / TAU)
        grad_rows(c)[...] = jnp.transpose(grad).astype(jnp.bfloat16)
        for m in (2, 1) if c < relayed else (3, 2, 1):
            grads[c][m - 1].start()

    def pull(k):
        rows = slice(k * span, (k + 1) * span)
        pull_scr[rows, :] = jnp.dot(p_scr[rows, :], qs_scr[...], preferred_element_type=jnp.float32).astype(jnp.bfloat16)
        pulls[k].start()

    def renew(k):
        pulls[k].wait_recv()
        for i in range(span // BCH):
            rows = slice(k * span + i * BCH, k * span + (i + 1) * BCH)
            both = pull_scr[rows, :].astype(jnp.float32) + pull_in_scr[rows, :].astype(jnp.float32)
            fresh = bank_ref[rows, :].astype(jnp.float32) + eta * both
            fresh = fresh * lax.rsqrt(jnp.mean(fresh * fresh, axis=1, keepdims=True) + EPS)
            new_ref[rows, :] = fresh.astype(jnp.bfloat16)

    q_load.wait()
    for c in range(chunks):
        compute(c)
    pick_keys()
    level(0)
    combine(0)
    level(1)
    combine(1)
    level(2)
    level(3)
    drain(pos_scr.at[0:3], pos_recv.at[0])
    pos_all = pos_scr[0]
    for j in range(1, 4):
        pos_all = pos_all + pos_scr[j]
    combine(2)
    settled = [settle(0, pos_all)]
    finalize(0, *settled[0])
    settled.append(settle(1, pos_all))
    combine(3)
    finalize(1, *settled[1])
    settled.append(settle(2, pos_all))
    finalize(2, *settled[2])
    settled.append(settle(3, pos_all))
    relay(0)
    finalize(3, *settled[3])
    for k in range(sends):
        pull(k)
    for k in range(sends):
        renew(k)

    drain(grad_ref.at[:, 0:qdev * 3 // 4 - relayed * TILE // 2, :], grad_recv.at[0])
    drain(stats_scr.at[:, 0:3], stats_send)
    drain(level_scr.at[:, 0], level_send)
    drain(pos_scr.at[0:3], pos_send)
    drain(square_scr, square_send)
    drain(mirror_scr.at[:, 0], mirror_send)
    drain(grad_ref.at[:, 0:qdev * 3 // 4, :], grad_send)
    drain(pull_scr, pull_send)


def fused(bank, queries, keys, labels, mask_tiles):
    n = lax.axis_size("bank")
    qdev, width = queries.shape
    bdev = bank.shape[0]
    chunks = qdev // QCH
    eta = 0.25 * (bdev * n) / (qdev * lax.axis_size("batch"))
    vmem = pl.BlockSpec(memory_space=pltpu.VMEM)
    hbm = pl.BlockSpec(memory_space=pltpu.HBM)
    dma = pltpu.SemaphoreType.DMA
    new_bank, grad, loss = pl.pallas_call(
        functools.partial(step_kernel, n, eta),
        out_shape=(
            pltpu.VMEM((bdev, width), jnp.bfloat16),
            pltpu.VMEM((2, qdev, TILE), jnp.bfloat16),
            pltpu.VMEM((n, TILE), jnp.float32),
        ),
        in_specs=[hbm] * 5,
        out_specs=(vmem, vmem, vmem),
        scratch_shapes=[
            pltpu.VMEM(mask_tiles.shape, jnp.int32),
            pltpu.VMEM((bdev, width), jnp.bfloat16),
            pltpu.VMEM((qdev, width), jnp.bfloat16),
            pltpu.VMEM((qdev, width), jnp.bfloat16),
            pltpu.VMEM((n, TILE), jnp.int32),
            pltpu.VMEM((2, bdev, QCH), jnp.float32),
            pltpu.VMEM((bdev, qdev), jnp.bfloat16),
            pltpu.VMEM((width, bdev), jnp.bfloat16),
            pltpu.VMEM((n, bdev // TILE, TILE), jnp.float32),
            pltpu.VMEM((qdev, width), jnp.bfloat16),
            pltpu.VMEM((chunks, TILE, TILE), jnp.float32),
            pltpu.VMEM((chunks, 4, 4, TILE), jnp.float32),
            pltpu.VMEM((chunks, 2, 4, TILE), jnp.float32),
            pltpu.VMEM((4, 8, TILE), jnp.float32),
            pltpu.VMEM((qdev, width), jnp.bfloat16),
            pltpu.VMEM((chunks, 4, TILE, TILE), jnp.bfloat16),
            pltpu.VMEM((chunks, 3, TILE, TILE), jnp.bfloat16),
            pltpu.VMEM((chunks, 2, TILE, TILE), jnp.bfloat16),
            pltpu.VMEM((bdev, width), jnp.bfloat16),
            pltpu.VMEM((bdev, width), jnp.bfloat16),
            dma((8,)), dma((2,)), dma((7,)),
            dma((1,)), dma((chunks,)), dma((chunks,)), dma((chunks,)), dma((chunks,)), dma((3,)), dma((4,)),
        ],
        compiler_params=pltpu.CompilerParams(
            collective_id=0, has_side_effects=True, vmem_limit_bytes=60 * 1024 * 1024
        ),
    )(mask_tiles, bank, queries, keys, labels.reshape(n, TILE))
    new_bank, query_grad, loss = finish(new_bank, grad, loss)
    return (new_bank, query_grad, loss.reshape(qdev))


def finish_kernel(bank_in, grad_in, loss_in, bank_out, grad_out, loss_out, out_scr, sems):
    qdev = grad_out.shape[0]
    steps = 4
    rows = qdev // steps
    copies = [pltpu.make_async_copy(bank_in, bank_out, sems.at[0]), pltpu.make_async_copy(loss_in, loss_out, sems.at[1])]
    for c in copies: c.start()
    for i in range(steps):
        r = slice(i * rows, (i + 1) * rows)
        out_scr[r, :TILE] = grad_in[0, r, :].astype(jnp.float32)
        out_scr[r, TILE:] = grad_in[1, r, :].astype(jnp.float32)
        copies.append(pltpu.make_async_copy(out_scr.at[r, :], grad_out.at[r, :], sems.at[2 + i]))
        copies[-1].start()
    for c in copies: c.wait()


def finish(new_bank, grad, loss):
    bdev, width = new_bank.shape
    qdev = grad.shape[1]
    hbm = pl.BlockSpec(memory_space=pltpu.HBM)
    return pl.pallas_call(
        finish_kernel,
        out_shape=(
            jax.ShapeDtypeStruct((bdev, width), jnp.bfloat16),
            jax.ShapeDtypeStruct((qdev, width), jnp.float32),
            jax.ShapeDtypeStruct(loss.shape, jnp.float32),
        ),
        in_specs=[pl.BlockSpec(memory_space=pltpu.VMEM)] * 3,
        out_specs=(hbm, hbm, hbm),
        scratch_shapes=[pltpu.VMEM((qdev, width), jnp.float32), pltpu.SemaphoreType.DMA((6,))],
        compiler_params=pltpu.CompilerParams(vmem_limit_bytes=16 * 1024 * 1024),
    )(new_bank, grad, loss)


def on_device(bank, queries, keys, labels, mask_tiles):
    n = lax.axis_size("bank")
    fits = (
        n == 8
        and queries.shape == (n * TILE, 2 * TILE)
        and bank.shape[0] % BCH == 0
        and lax.axis_size("batch") == 2
    )
    return (fused if fits else general)(bank, queries, keys, labels, mask_tiles)


def solution(mesh):
    return jax.shard_map(
        on_device,
        mesh=mesh,
        in_specs=(
            P(("parts", "bank"), None),
            P(("parts", "batch"), None),
            P(("parts", "batch"), None),
            P(("parts", "batch")),
            P("parts", None),
        ),
        out_specs=(P(("parts", "bank"), None), P(("parts", "batch"), None), P(("parts", "batch"))),
        check_vma=False,
    )
```

```python
import functools
import math

import jax
import jax.numpy as jnp
from jax import lax
from jax.experimental import pallas as pl
from jax.experimental.pallas import tpu as pltpu
from jax.sharding import PartitionSpec as P

TILE = 128


TAU = 0.12
NEG = -1e30
FLOOR = -1e29
EPS = 1e-06
LOG2E = math.log2(math.e)
LN2 = math.log(2.0)
SCALE2 = LOG2E / TAU
QCH = 256
BCH = 256
MESH = pl.DeviceIdType.MESH


def masked_scores(rows_q, rows_k, mask_rows, first):
    s = jnp.einsum("qd,kd->qk", rows_q, rows_k, preferred_element_type=jnp.float32) / TAU
    nq, nk = s.shape
    ids = first + jnp.arange(nk // TILE, dtype=jnp.int32)
    hit = jnp.any(mask_rows[:, :, None] == ids[None, None, :], axis=1)
    live = jnp.broadcast_to(
        jnp.logical_not(hit)[:, None, :, None], (nq // TILE, TILE, nk // TILE, TILE)
    ).reshape(nq, nk)
    return (jnp.where(live, s, NEG), live)


def general(bank, queries, keys, labels, mask_tiles):
    qdev = queries.shape[0]
    bdev = bank.shape[0]
    total_bank = bdev * lax.axis_size("bank")
    total_query = qdev * lax.axis_size("batch")
    eta = 0.25 * total_bank / total_query
    mine = lax.axis_index("batch")
    first = lax.axis_index("bank") * (bdev // TILE)
    all_keys = lax.all_gather(keys, "batch", axis=0, tiled=True)
    key_rows = jnp.take(all_keys, labels, axis=0)
    pos = jnp.sum(queries.astype(jnp.float32) * key_rows.astype(jnp.float32), axis=1) / TAU
    own_mask = lax.dynamic_slice_in_dim(mask_tiles, mine * (qdev // TILE), qdev // TILE, 0)
    scores, live = masked_scores(queries, bank, own_mask, first)
    top = lax.pmax(jnp.max(scores, axis=1), "bank")
    part_sum = jnp.sum(jnp.where(live, jnp.exp(scores - top[:, None]), 0.0), axis=1)
    total = lax.psum(part_sum, "bank")
    high = jnp.maximum(top, pos)
    lse = high + jnp.log(total * jnp.exp(top - high) + jnp.exp(pos - high))
    loss = lse - pos
    probs = jnp.exp(scores - lse[:, None]).astype(jnp.bfloat16)
    neg_local = jnp.dot(probs, bank, preferred_element_type=jnp.float32)
    own_pull = jnp.einsum("qk,qd->kd", probs, queries, preferred_element_type=jnp.float32)
    neg = lax.psum(neg_local, "bank")
    query_grad = (neg + (jnp.exp(pos - lse) - 1.0)[:, None] * key_rows.astype(jnp.float32)) / TAU
    pull = lax.psum(own_pull.astype(jnp.bfloat16), "batch").astype(jnp.float32)
    fresh = bank.astype(jnp.float32) + eta * pull
    fresh = fresh * lax.rsqrt(jnp.mean(fresh * fresh, axis=1, keepdims=True) + EPS)
    return (fresh.astype(jnp.bfloat16), query_grad, loss)


def column(row):
    return jnp.transpose(jnp.broadcast_to(row, (TILE, TILE)))


def wide_column(row, width):
    return jnp.concatenate([column(row)] * (width // TILE), axis=1)


def step_kernel(
    n, eta, mask_hbm, bank_hbm, q_hbm, keys_hbm, labels_hbm,
    new_ref, grad_ref, loss_ref,
    mask_ref, bank_ref, q_ref, keys_ref, labels_ref,
    s_scr, p_scr, bankt_scr, bias_scr, keys_scr, key_t_scr, stats_scr, level_scr, pos_scr, qs_scr,
    stage_scr, square_scr, mirror_scr, pull_scr, pull_in_scr,
    in_sems, keys_sems, send_sems, pos_recv, stats_recv, level_recv, square_recv, mirror_recv, grad_recv, pull_recv,
):
    me = lax.axis_index("bank")
    mine = lax.axis_index("batch")
    other = 1 - mine
    bdev, width = bank_ref.shape
    qdev = q_ref.shape[0]
    tiles = bdev // TILE
    chunks = qdev // QCH
    parts = bdev // BCH
    listed = mask_ref.shape[1]
    first = me * tiles
    x = lax.rem(me, 2)
    zl = lax.rem(me // 2, 2)
    zh = me // 4
    quarter = zl * 2 + x

    relayed = 1
    pieces = 2
    piece = bdev // pieces
    mask_load = pltpu.make_async_copy(mask_hbm, mask_ref, in_sems.at[0])
    q_load = pltpu.make_async_copy(q_hbm, q_ref, in_sems.at[1])
    bank_loads = [
        pltpu.make_async_copy(bank_hbm.at[i * piece:(i + 1) * piece, :], bank_ref.at[i * piece:(i + 1) * piece, :], in_sems.at[4 + i])
        for i in range(pieces)]
    labels_load = pltpu.make_async_copy(labels_hbm, labels_ref, in_sems.at[2])
    keys_load = pltpu.make_async_copy(keys_hbm, keys_ref, in_sems.at[3])
    for load in [mask_load, q_load] + bank_loads:
        load.start()

    barrier = pltpu.get_barrier_semaphore()
    for d in range(1, n):
        pl.semaphore_signal(barrier, inc=1, device_id={"bank": lax.rem(me + d, n)}, device_id_type=MESH)
    pl.semaphore_signal(barrier, inc=1, device_id={"batch": other}, device_id_type=MESH)

    def peer(m):
        low = (1 - zl if m & 2 else zl) * 2 + (1 - x if m & 1 else x)
        return low, (1 - zh if m & 4 else zh) * 4 + low

    def to_bank(m, src, dst, send, recv):
        return pltpu.make_async_remote_copy(
            src_ref=src, dst_ref=dst, send_sem=send, recv_sem=recv,
            device_id={"bank": peer(m)[1]}, device_id_type=MESH)

    def to_core(src, dst, send, recv):
        return pltpu.make_async_remote_copy(
            src_ref=src, dst_ref=dst, send_sem=send, recv_sem=recv,
            device_id={"batch": other}, device_id_type=MESH)

    keys_copy = to_core(keys_hbm, keys_scr, keys_sems.at[0], keys_sems.at[1])
    def drain(ref, sem):
        pltpu.make_async_copy(ref, ref, sem).wait()

    stats_send, level_send, pos_send, square_send, mirror_send, grad_send, pull_send = [send_sems.at[i] for i in range(7)]
    stats = [[to_bank(m, stats_scr.at[c, quarter], stats_scr.at[c, quarter], stats_send, stats_recv.at[c])
              for m in range(1, 4)] for c in range(chunks)]
    levels = [to_bank(4, level_scr.at[c, zh], level_scr.at[c, zh], level_send, level_recv.at[c]) for c in range(chunks)]
    poses = [to_bank(m, pos_scr.at[quarter], pos_scr.at[quarter], pos_send, pos_recv.at[0]) for m in range(1, 4)]
    squares = [[to_bank(m, stage_scr.at[c, peer(m)[0]], square_scr.at[c, m - 1], square_send, square_recv.at[c])
                for m in range(1, 4)] for c in range(chunks)]
    mirrors = [to_bank(4, mirror_scr.at[c, zh], mirror_scr.at[c, zh], mirror_send, mirror_recv.at[c]) for c in range(chunks)]

    def grad_rows(c):
        return grad_ref.at[x, pl.ds(pl.multiple_of(c * QCH + zl * TILE, TILE), TILE), :]

    grads = [[to_bank(m, grad_rows(c), grad_rows(c), grad_send, grad_recv.at[1 + c if m == 2 and c < relayed else 0])
              for m in range(1, 4)] for c in range(chunks)]

    def came_rows(c):
        return grad_ref.at[x, pl.ds(pl.multiple_of(c * QCH + (1 - zl) * TILE, TILE), TILE), :]

    relays = [to_bank(1, came_rows(c), came_rows(c), grad_send, grad_recv.at[0]) for c in range(relayed)]

    def relay(c):
        drain(came_rows(c), grad_recv.at[1 + c])
        relays[c].start()
    sends = 4
    span = bdev // sends
    pulls = [to_core(pull_scr.at[k * span:(k + 1) * span, :], pull_in_scr.at[k * span:(k + 1) * span, :], pull_send, pull_recv.at[k])
             for k in range(sends)]

    mask_load.wait()
    ids = first + lax.broadcasted_iota(jnp.int32, (tiles, listed), 0)
    for b in range(qdev // TILE):
        hit = jnp.where(ids == mask_ref[pl.ds(mine * (qdev // TILE) + b, 1), :], 1.0, 0.0)
        bias_scr[b] = jnp.broadcast_to(jnp.max(hit, axis=1, keepdims=True), (tiles, TILE)) * NEG

    def compute(c):
        cols = slice(c * QCH, (c + 1) * QCH)
        bias = [jnp.concatenate([bias_scr[c * (QCH // TILE) + u, t:t + 1, :] for u in range(QCH // TILE)], axis=1) for t in range(tiles)]
        qc = q_ref[cols, :]
        top8 = jnp.full((8, QCH), FLOOR / SCALE2, jnp.float32)
        for k in range(parts):
            if c == 0 and k * BCH % piece == 0:
                bank_loads[k * BCH // piece].wait()
            s = lax.dot_general(bank_ref[k * BCH:(k + 1) * BCH, :], qc, (((1,), (1,)), ((), ())),
                                preferred_element_type=jnp.float32)
            s_scr[c % 2, k * BCH:(k + 1) * BCH, :] = s
            for t in range(BCH // TILE):
                part = s[t * TILE:(t + 1) * TILE, :].reshape(TILE // 8, 8, QCH)
                top8 = jnp.maximum(top8, jnp.max(part, axis=0) + bias[k * (BCH // TILE) + t])
            if c == 0:
                bankt_scr[:, k * BCH:(k + 1) * BCH] = jnp.transpose(bank_ref[k * BCH:(k + 1) * BCH, :])
        top = jnp.max(top8, axis=0, keepdims=True) * SCALE2
        sum8 = jnp.zeros((8, QCH), jnp.float32)
        for t in range(tiles):
            rows = slice(t * TILE, (t + 1) * TILE)
            p = jnp.exp2(s_scr[c % 2, rows, :] * SCALE2 - (top - bias[t]))
            sum8 = sum8 + jnp.sum(p.reshape(TILE // 8, 8, QCH), axis=0)
            p_scr[rows, cols] = p.astype(jnp.bfloat16)
        total = jnp.sum(sum8, axis=0, keepdims=True)
        for u in range(QCH // TILE):
            stats_scr[c, quarter, u:u + 1, :] = top[:, u * TILE:(u + 1) * TILE]
            stats_scr[c, quarter, 2 + u:3 + u, :] = total[:, u * TILE:(u + 1) * TILE]
        if c == 0:
            labels_load.start()
            keys_load.start()
            pl.semaphore_wait(barrier, n)
        for copy in stats[c]:
            copy.start()
        neg = jnp.dot(bankt_scr[...], p_scr[:, cols], preferred_element_type=jnp.float32).astype(jnp.bfloat16)
        for u in range(2):
            for h in range(2):
                stage_scr[c, u * 2 + h] = neg[h * TILE:(h + 1) * TILE, u * TILE:(u + 1) * TILE]
        for m in (3, 2, 1):
            squares[c][m - 1].start()
        if c == 0:
            keys_copy.start()

    def pick_keys():
        labels_load.wait()
        keys_load.wait()
        keys_copy.wait()
        half = pl.ds(pl.multiple_of(x * TILE, TILE), TILE)
        row_ids = lax.broadcasted_iota(jnp.int32, (qdev, TILE), 0)
        row8 = lax.broadcasted_iota(jnp.int32, (8, TILE), 0)

        def picked(table, labels):
            hot = jnp.where(row_ids == labels, 1.0, 0.0).astype(jnp.bfloat16)
            return lax.dot_general(hot, table, (((0,), (0,)), ((), ())), preferred_element_type=jnp.float32)

        tile = jnp.zeros((8, TILE), jnp.float32)
        for c in range(chunks):
            labels = labels_ref[pl.ds(2 * c + zl, 1), :]
            rows = picked(keys_ref[:, half], labels - mine * qdev) + picked(keys_scr[:, half], labels - other * qdev)
            key_t = jnp.transpose(rows)
            key_t_scr[c] = key_t
            own = pl.ds(pl.multiple_of(c * QCH + zl * TILE, TILE), TILE)
            q_t = jnp.transpose(q_ref[own, half].astype(jnp.float32))
            pos = jnp.sum(key_t * q_t, axis=0, keepdims=True) * SCALE2
            tile = jnp.where(row8 == 2 * c + zl, pos, tile)
        pos_scr[quarter] = tile
        for copy in poses:
            copy.start()

    def level(c):
        drain(stats_scr.at[c, 0:3], stats_recv.at[c])
        top = stats_scr[c, 0, 0:2, :]
        for b in range(1, 4):
            top = jnp.maximum(top, stats_scr[c, b, 0:2, :])
        total = stats_scr[c, 0, 2:4, :] * jnp.exp2(stats_scr[c, 0, 0:2, :] - top)
        for b in range(1, 4):
            total = total + stats_scr[c, b, 2:4, :] * jnp.exp2(stats_scr[c, b, 0:2, :] - top)
        level_scr[c, zh, 0:2, :] = top
        level_scr[c, zh, 2:4, :] = total
        levels[c].start()

    def combine(c):
        drain(square_scr.at[c], square_recv.at[c])
        both = level_scr[c, zh, pl.ds(zl, 1), :]
        total = None
        for m in range(4):
            piece = stage_scr[c, quarter] if m == 0 else square_scr[c, m - 1]
            term = piece.astype(jnp.float32) * jnp.exp2(stats_scr[c, peer(m)[0], pl.ds(zl, 1), :] - both)
            total = term if m == 0 else total + term
        mirror_scr[c, zh] = total.astype(jnp.bfloat16)
        mirrors[c].start()

    def settle(c, pos_all):
        drain(level_scr.at[c, 0], level_recv.at[c])
        pos = pos_all[2 * c:2 * c + 2, :]
        tops = [level_scr[c, side, 0:2, :] for side in range(2)]
        high = jnp.maximum(pos, jnp.maximum(tops[0], tops[1]))
        total = jnp.exp2(pos - high)
        for side in range(2):
            total = total + level_scr[c, side, 2:4, :] * jnp.exp2(tops[side] - high)
        lse = high + jnp.log(total) * LOG2E
        loss_ref[2 * c:2 * c + 2, :] = (lse - pos) * LN2
        alpha = jnp.exp2(stats_scr[c, quarter, 0:2, :] - lse)
        for u in range(2):
            rows = slice(c * QCH + u * TILE, c * QCH + (u + 1) * TILE)
            qs_scr[rows, :] = (q_ref[rows, :].astype(jnp.float32) * wide_column(alpha[u:u + 1, :], width)).astype(jnp.bfloat16)
        return jnp.where(zl == 0, lse[0:1, :], lse[1:2, :]), jnp.where(zl == 0, pos[0:1, :], pos[1:2, :])

    def finalize(c, lse, pos):
        drain(mirror_scr.at[c, 0], mirror_recv.at[c])
        neg = None
        for side in range(2):
            term = mirror_scr[c, side].astype(jnp.float32) * jnp.exp2(level_scr[c, side, pl.ds(zl, 1), :] - lse)
            neg = term if neg is None else neg + term
        grad = (neg + (jnp.exp2(pos - lse) - 1.0) * key_t_scr[c]) * (1.0 / TAU)
        grad_rows(c)[...] = jnp.transpose(grad).astype(jnp.bfloat16)
        for m in (2, 1) if c < relayed else (3, 2, 1):
            grads[c][m - 1].start()

    def pull(k):
        rows = slice(k * span, (k + 1) * span)
        pull_scr[rows, :] = jnp.dot(p_scr[rows, :], qs_scr[...], preferred_element_type=jnp.float32).astype(jnp.bfloat16)
        pulls[k].start()

    def renew(k):
        pulls[k].wait_recv()
        for i in range(span // BCH):
            rows = slice(k * span + i * BCH, k * span + (i + 1) * BCH)
            both = pull_scr[rows, :].astype(jnp.float32) + pull_in_scr[rows, :].astype(jnp.float32)
            fresh = bank_ref[rows, :].astype(jnp.float32) + eta * both
            fresh = fresh * lax.rsqrt(jnp.mean(fresh * fresh, axis=1, keepdims=True) + EPS)
            new_ref[rows, :] = fresh.astype(jnp.bfloat16)

    q_load.wait()
    for c in range(chunks):
        compute(c)
    pick_keys()
    level(0)
    combine(0)
    level(1)
    combine(1)
    level(2)
    combine(2)
    drain(pos_scr.at[0:3], pos_recv.at[0])
    pos_all = pos_scr[0]
    for j in range(1, 4):
        pos_all = pos_all + pos_scr[j]
    settled = [settle(0, pos_all)]
    finalize(0, *settled[0])
    settled.append(settle(1, pos_all))
    level(3)
    combine(3)
    finalize(1, *settled[1])
    settled.append(settle(2, pos_all))
    finalize(2, *settled[2])
    settled.append(settle(3, pos_all))
    relay(0)
    finalize(3, *settled[3])
    for k in range(sends):
        pull(k)
    for k in range(sends):
        renew(k)

    drain(grad_ref.at[:, 0:qdev * 3 // 4 - relayed * TILE // 2, :], grad_recv.at[0])
    drain(stats_scr.at[:, 0:3], stats_send)
    drain(level_scr.at[:, 0], level_send)
    drain(pos_scr.at[0:3], pos_send)
    drain(square_scr, square_send)
    drain(mirror_scr.at[:, 0], mirror_send)
    drain(grad_ref.at[:, 0:qdev * 3 // 4, :], grad_send)
    drain(pull_scr, pull_send)


def fused(bank, queries, keys, labels, mask_tiles):
    n = lax.axis_size("bank")
    qdev, width = queries.shape
    bdev = bank.shape[0]
    chunks = qdev // QCH
    eta = 0.25 * (bdev * n) / (qdev * lax.axis_size("batch"))
    vmem = pl.BlockSpec(memory_space=pltpu.VMEM)
    hbm = pl.BlockSpec(memory_space=pltpu.HBM)
    dma = pltpu.SemaphoreType.DMA
    new_bank, grad, loss = pl.pallas_call(
        functools.partial(step_kernel, n, eta),
        out_shape=(
            pltpu.VMEM((bdev, width), jnp.bfloat16),
            pltpu.VMEM((2, qdev, TILE), jnp.bfloat16),
            pltpu.VMEM((n, TILE), jnp.float32),
        ),
        in_specs=[hbm] * 5,
        out_specs=(vmem, vmem, vmem),
        scratch_shapes=[
            pltpu.VMEM(mask_tiles.shape, jnp.int32),
            pltpu.VMEM((bdev, width), jnp.bfloat16),
            pltpu.VMEM((qdev, width), jnp.bfloat16),
            pltpu.VMEM((qdev, width), jnp.bfloat16),
            pltpu.VMEM((n, TILE), jnp.int32),
            pltpu.VMEM((2, bdev, QCH), jnp.float32),
            pltpu.VMEM((bdev, qdev), jnp.bfloat16),
            pltpu.VMEM((width, bdev), jnp.bfloat16),
            pltpu.VMEM((n, bdev // TILE, TILE), jnp.float32),
            pltpu.VMEM((qdev, width), jnp.bfloat16),
            pltpu.VMEM((chunks, TILE, TILE), jnp.float32),
            pltpu.VMEM((chunks, 4, 4, TILE), jnp.float32),
            pltpu.VMEM((chunks, 2, 4, TILE), jnp.float32),
            pltpu.VMEM((4, 8, TILE), jnp.float32),
            pltpu.VMEM((qdev, width), jnp.bfloat16),
            pltpu.VMEM((chunks, 4, TILE, TILE), jnp.bfloat16),
            pltpu.VMEM((chunks, 3, TILE, TILE), jnp.bfloat16),
            pltpu.VMEM((chunks, 2, TILE, TILE), jnp.bfloat16),
            pltpu.VMEM((bdev, width), jnp.bfloat16),
            pltpu.VMEM((bdev, width), jnp.bfloat16),
            dma((8,)), dma((2,)), dma((7,)),
            dma((1,)), dma((chunks,)), dma((chunks,)), dma((chunks,)), dma((chunks,)), dma((3,)), dma((4,)),
        ],
        compiler_params=pltpu.CompilerParams(
            collective_id=0, has_side_effects=True, vmem_limit_bytes=60 * 1024 * 1024
        ),
    )(mask_tiles, bank, queries, keys, labels.reshape(n, TILE))
    new_bank, query_grad, loss = finish(new_bank, grad, loss)
    return (new_bank, query_grad, loss.reshape(qdev))


def finish_kernel(bank_in, grad_in, loss_in, bank_out, grad_out, loss_out, out_scr, sems):
    qdev = grad_out.shape[0]
    steps = 4
    rows = qdev // steps
    copies = [pltpu.make_async_copy(bank_in, bank_out, sems.at[0]), pltpu.make_async_copy(loss_in, loss_out, sems.at[1])]
    for c in copies: c.start()
    for i in range(steps):
        r = slice(i * rows, (i + 1) * rows)
        out_scr[r, :TILE] = grad_in[0, r, :].astype(jnp.float32)
        out_scr[r, TILE:] = grad_in[1, r, :].astype(jnp.float32)
        copies.append(pltpu.make_async_copy(out_scr.at[r, :], grad_out.at[r, :], sems.at[2 + i]))
        copies[-1].start()
    for c in copies: c.wait()


def finish(new_bank, grad, loss):
    bdev, width = new_bank.shape
    qdev = grad.shape[1]
    hbm = pl.BlockSpec(memory_space=pltpu.HBM)
    return pl.pallas_call(
        finish_kernel,
        out_shape=(
            jax.ShapeDtypeStruct((bdev, width), jnp.bfloat16),
            jax.ShapeDtypeStruct((qdev, width), jnp.float32),
            jax.ShapeDtypeStruct(loss.shape, jnp.float32),
        ),
        in_specs=[pl.BlockSpec(memory_space=pltpu.VMEM)] * 3,
        out_specs=(hbm, hbm, hbm),
        scratch_shapes=[pltpu.VMEM((qdev, width), jnp.float32), pltpu.SemaphoreType.DMA((6,))],
        compiler_params=pltpu.CompilerParams(vmem_limit_bytes=16 * 1024 * 1024),
    )(new_bank, grad, loss)


def on_device(bank, queries, keys, labels, mask_tiles):
    n = lax.axis_size("bank")
    fits = (
        n == 8
        and queries.shape == (n * TILE, 2 * TILE)
        and bank.shape[0] % BCH == 0
        and lax.axis_size("batch") == 2
    )
    return (fused if fits else general)(bank, queries, keys, labels, mask_tiles)


def solution(mesh):
    return jax.shard_map(
        on_device,
        mesh=mesh,
        in_specs=(
            P(("parts", "bank"), None),
            P(("parts", "batch"), None),
            P(("parts", "batch"), None),
            P(("parts", "batch")),
            P("parts", None),
        ),
        out_specs=(P(("parts", "bank"), None), P(("parts", "batch"), None), P(("parts", "batch"))),
        check_vma=False,
    )
```

```python
import functools
import math

import jax
import jax.numpy as jnp
from jax import lax
from jax.experimental import pallas as pl
from jax.experimental.pallas import tpu as pltpu
from jax.sharding import PartitionSpec as P

TILE = 128


TAU = 0.12
NEG = -1e30
FLOOR = -1e29
EPS = 1e-06
LOG2E = math.log2(math.e)
LN2 = math.log(2.0)
SCALE2 = LOG2E / TAU
QCH = 256
BCH = 256
MESH = pl.DeviceIdType.MESH


def masked_scores(rows_q, rows_k, mask_rows, first):
    s = jnp.einsum("qd,kd->qk", rows_q, rows_k, preferred_element_type=jnp.float32) / TAU
    nq, nk = s.shape
    ids = first + jnp.arange(nk // TILE, dtype=jnp.int32)
    hit = jnp.any(mask_rows[:, :, None] == ids[None, None, :], axis=1)
    live = jnp.broadcast_to(
        jnp.logical_not(hit)[:, None, :, None], (nq // TILE, TILE, nk // TILE, TILE)
    ).reshape(nq, nk)
    return (jnp.where(live, s, NEG), live)


def general(bank, queries, keys, labels, mask_tiles):
    qdev = queries.shape[0]
    bdev = bank.shape[0]
    total_bank = bdev * lax.axis_size("bank")
    total_query = qdev * lax.axis_size("batch")
    eta = 0.25 * total_bank / total_query
    mine = lax.axis_index("batch")
    first = lax.axis_index("bank") * (bdev // TILE)
    all_keys = lax.all_gather(keys, "batch", axis=0, tiled=True)
    key_rows = jnp.take(all_keys, labels, axis=0)
    pos = jnp.sum(queries.astype(jnp.float32) * key_rows.astype(jnp.float32), axis=1) / TAU
    own_mask = lax.dynamic_slice_in_dim(mask_tiles, mine * (qdev // TILE), qdev // TILE, 0)
    scores, live = masked_scores(queries, bank, own_mask, first)
    top = lax.pmax(jnp.max(scores, axis=1), "bank")
    part_sum = jnp.sum(jnp.where(live, jnp.exp(scores - top[:, None]), 0.0), axis=1)
    total = lax.psum(part_sum, "bank")
    high = jnp.maximum(top, pos)
    lse = high + jnp.log(total * jnp.exp(top - high) + jnp.exp(pos - high))
    loss = lse - pos
    probs = jnp.exp(scores - lse[:, None]).astype(jnp.bfloat16)
    neg_local = jnp.dot(probs, bank, preferred_element_type=jnp.float32)
    own_pull = jnp.einsum("qk,qd->kd", probs, queries, preferred_element_type=jnp.float32)
    neg = lax.psum(neg_local, "bank")
    query_grad = (neg + (jnp.exp(pos - lse) - 1.0)[:, None] * key_rows.astype(jnp.float32)) / TAU
    pull = lax.psum(own_pull.astype(jnp.bfloat16), "batch").astype(jnp.float32)
    fresh = bank.astype(jnp.float32) + eta * pull
    fresh = fresh * lax.rsqrt(jnp.mean(fresh * fresh, axis=1, keepdims=True) + EPS)
    return (fresh.astype(jnp.bfloat16), query_grad, loss)


def column(row):
    return jnp.transpose(jnp.broadcast_to(row, (TILE, TILE)))


def wide_column(row, width):
    return jnp.concatenate([column(row)] * (width // TILE), axis=1)


def step_kernel(
    n, eta, mask_hbm, bank_hbm, q_hbm, keys_hbm, labels_hbm,
    new_ref, grad_ref, loss_ref,
    mask_ref, bank_ref, q_ref, keys_ref, labels_ref,
    s_scr, p_scr, bankt_scr, bias_scr, keys_scr, key_t_scr, stats_scr, level_scr, pos_scr, qs_scr,
    stage_scr, square_scr, mirror_scr, pull_scr, pull_in_scr,
    in_sems, keys_sems, send_sems, pos_recv, stats_recv, level_recv, square_recv, mirror_recv, grad_recv, pull_recv,
):
    me = lax.axis_index("bank")
    mine = lax.axis_index("batch")
    other = 1 - mine
    bdev, width = bank_ref.shape
    qdev = q_ref.shape[0]
    tiles = bdev // TILE
    chunks = qdev // QCH
    parts = bdev // BCH
    listed = mask_ref.shape[1]
    first = me * tiles
    x = lax.rem(me, 2)
    zl = lax.rem(me // 2, 2)
    zh = me // 4
    quarter = zl * 2 + x

    relayed = 1
    pieces = 2
    piece = bdev // pieces
    mask_load = pltpu.make_async_copy(mask_hbm, mask_ref, in_sems.at[0])
    q_load = pltpu.make_async_copy(q_hbm, q_ref, in_sems.at[1])
    bank_loads = [
        pltpu.make_async_copy(bank_hbm.at[i * piece:(i + 1) * piece, :], bank_ref.at[i * piece:(i + 1) * piece, :], in_sems.at[4 + i])
        for i in range(pieces)]
    labels_load = pltpu.make_async_copy(labels_hbm, labels_ref, in_sems.at[2])
    keys_load = pltpu.make_async_copy(keys_hbm, keys_ref, in_sems.at[3])
    for load in [mask_load, q_load] + bank_loads + [labels_load, keys_load]:
        load.start()

    barrier = pltpu.get_barrier_semaphore()
    for d in range(1, n):
        pl.semaphore_signal(barrier, inc=1, device_id={"bank": lax.rem(me + d, n)}, device_id_type=MESH)
    pl.semaphore_signal(barrier, inc=1, device_id={"batch": other}, device_id_type=MESH)

    def peer(m):
        low = (1 - zl if m & 2 else zl) * 2 + (1 - x if m & 1 else x)
        return low, (1 - zh if m & 4 else zh) * 4 + low

    def to_bank(m, src, dst, send, recv):
        return pltpu.make_async_remote_copy(
            src_ref=src, dst_ref=dst, send_sem=send, recv_sem=recv,
            device_id={"bank": peer(m)[1]}, device_id_type=MESH)

    def to_core(src, dst, send, recv):
        return pltpu.make_async_remote_copy(
            src_ref=src, dst_ref=dst, send_sem=send, recv_sem=recv,
            device_id={"batch": other}, device_id_type=MESH)

    keys_copy = to_core(keys_ref, keys_scr, keys_sems.at[0], keys_sems.at[1])
    def drain(ref, sem):
        pltpu.make_async_copy(ref, ref, sem).wait()

    stats_send, level_send, pos_send, square_send, mirror_send, grad_send, pull_send = [send_sems.at[i] for i in range(7)]
    stats = [[to_bank(m, stats_scr.at[c, quarter], stats_scr.at[c, quarter], stats_send, stats_recv.at[c])
              for m in range(1, 4)] for c in range(chunks)]
    levels = [to_bank(4, level_scr.at[c, zh], level_scr.at[c, zh], level_send, level_recv.at[c]) for c in range(chunks)]
    poses = [to_bank(m, pos_scr.at[quarter], pos_scr.at[quarter], pos_send, pos_recv.at[0]) for m in range(1, 4)]
    squares = [[to_bank(m, stage_scr.at[c, peer(m)[0]], square_scr.at[c, m - 1], square_send, square_recv.at[c])
                for m in range(1, 4)] for c in range(chunks)]
    mirrors = [to_bank(4, mirror_scr.at[c, zh], mirror_scr.at[c, zh], mirror_send, mirror_recv.at[c]) for c in range(chunks)]

    def grad_rows(c):
        return grad_ref.at[x, pl.ds(pl.multiple_of(c * QCH + zl * TILE, TILE), TILE), :]

    grads = [[to_bank(m, grad_rows(c), grad_rows(c), grad_send, grad_recv.at[1 + c if m == 2 and c < relayed else 0])
              for m in range(1, 4)] for c in range(chunks)]

    def came_rows(c):
        return grad_ref.at[x, pl.ds(pl.multiple_of(c * QCH + (1 - zl) * TILE, TILE), TILE), :]

    relays = [to_bank(1, came_rows(c), came_rows(c), grad_send, grad_recv.at[0]) for c in range(relayed)]

    def relay(c):
        drain(came_rows(c), grad_recv.at[1 + c])
        relays[c].start()
    sends = 4
    span = bdev // sends
    pulls = [to_core(pull_scr.at[k * span:(k + 1) * span, :], pull_in_scr.at[k * span:(k + 1) * span, :], pull_send, pull_recv.at[k])
             for k in range(sends)]

    mask_load.wait()
    ids = first + lax.broadcasted_iota(jnp.int32, (tiles, listed), 0)
    for b in range(qdev // TILE):
        hit = jnp.where(ids == mask_ref[pl.ds(mine * (qdev // TILE) + b, 1), :], 1.0, 0.0)
        bias_scr[b] = jnp.broadcast_to(jnp.max(hit, axis=1, keepdims=True), (tiles, TILE)) * NEG

    def score(c):
        cols = slice(c * QCH, (c + 1) * QCH)
        bias = [jnp.concatenate([bias_scr[c * (QCH // TILE) + u, t:t + 1, :] for u in range(QCH // TILE)], axis=1) for t in range(tiles)]
        qc = q_ref[cols, :]
        top8 = jnp.full((8, QCH), FLOOR / SCALE2, jnp.float32)
        for k in range(parts):
            if c == 0 and k * BCH % piece == 0:
                bank_loads[k * BCH // piece].wait()
            s = lax.dot_general(bank_ref[k * BCH:(k + 1) * BCH, :], qc, (((1,), (1,)), ((), ())),
                                preferred_element_type=jnp.float32)
            s_scr[c % 2, k * BCH:(k + 1) * BCH, :] = s
            for t in range(BCH // TILE):
                part = s[t * TILE:(t + 1) * TILE, :].reshape(TILE // 8, 8, QCH)
                top8 = jnp.maximum(top8, jnp.max(part, axis=0) + bias[k * (BCH // TILE) + t])
            if c == 0:
                bankt_scr[:, k * BCH:(k + 1) * BCH] = jnp.transpose(bank_ref[k * BCH:(k + 1) * BCH, :])
        top = jnp.max(top8, axis=0, keepdims=True) * SCALE2
        sum8 = jnp.zeros((8, QCH), jnp.float32)
        for t in range(tiles):
            rows = slice(t * TILE, (t + 1) * TILE)
            p = jnp.exp2(s_scr[c % 2, rows, :] * SCALE2 - (top - bias[t]))
            sum8 = sum8 + jnp.sum(p.reshape(TILE // 8, 8, QCH), axis=0)
            p_scr[rows, cols] = p.astype(jnp.bfloat16)
        total = jnp.sum(sum8, axis=0, keepdims=True)
        for u in range(QCH // TILE):
            stats_scr[c, quarter, u:u + 1, :] = top[:, u * TILE:(u + 1) * TILE]
            stats_scr[c, quarter, 2 + u:3 + u, :] = total[:, u * TILE:(u + 1) * TILE]

    def weigh(c):
        cols = slice(c * QCH, (c + 1) * QCH)
        neg = jnp.dot(bankt_scr[...], p_scr[:, cols], preferred_element_type=jnp.float32).astype(jnp.bfloat16)
        for u in range(2):
            for h in range(2):
                stage_scr[c, u * 2 + h] = neg[h * TILE:(h + 1) * TILE, u * TILE:(u + 1) * TILE]

    def send_stats(c):
        for copy in stats[c]:
            copy.start()

    def send_squares(c):
        for m in (3, 2, 1):
            squares[c][m - 1].start()

    def pick_keys():
        half = pl.ds(pl.multiple_of(x * TILE, TILE), TILE)
        row_ids = lax.broadcasted_iota(jnp.int32, (qdev, TILE), 0)
        row8 = lax.broadcasted_iota(jnp.int32, (8, TILE), 0)

        def picked(table, labels):
            hot = jnp.where(row_ids == labels, 1.0, 0.0).astype(jnp.bfloat16)
            return lax.dot_general(hot, table, (((0,), (0,)), ((), ())), preferred_element_type=jnp.float32)

        tile = jnp.zeros((8, TILE), jnp.float32)
        for c in range(chunks):
            labels = labels_ref[pl.ds(2 * c + zl, 1), :]
            rows = picked(keys_ref[:, half], labels - mine * qdev) + picked(keys_scr[:, half], labels - other * qdev)
            key_t = jnp.transpose(rows)
            key_t_scr[c] = key_t
            own = pl.ds(pl.multiple_of(c * QCH + zl * TILE, TILE), TILE)
            q_t = jnp.transpose(q_ref[own, half].astype(jnp.float32))
            pos = jnp.sum(key_t * q_t, axis=0, keepdims=True) * SCALE2
            tile = jnp.where(row8 == 2 * c + zl, pos, tile)
        pos_scr[quarter] = tile

    def level(c):
        drain(stats_scr.at[c, 0:3], stats_recv.at[c])
        top = stats_scr[c, 0, 0:2, :]
        for b in range(1, 4):
            top = jnp.maximum(top, stats_scr[c, b, 0:2, :])
        total = stats_scr[c, 0, 2:4, :] * jnp.exp2(stats_scr[c, 0, 0:2, :] - top)
        for b in range(1, 4):
            total = total + stats_scr[c, b, 2:4, :] * jnp.exp2(stats_scr[c, b, 0:2, :] - top)
        level_scr[c, zh, 0:2, :] = top
        level_scr[c, zh, 2:4, :] = total
        levels[c].start()

    def combine(c):
        drain(square_scr.at[c], square_recv.at[c])
        both = level_scr[c, zh, pl.ds(zl, 1), :]
        total = None
        for m in range(4):
            piece = stage_scr[c, quarter] if m == 0 else square_scr[c, m - 1]
            term = piece.astype(jnp.float32) * jnp.exp2(stats_scr[c, peer(m)[0], pl.ds(zl, 1), :] - both)
            total = term if m == 0 else total + term
        mirror_scr[c, zh] = total.astype(jnp.bfloat16)
        mirrors[c].start()

    def settle(c, pos_all):
        drain(level_scr.at[c, 0], level_recv.at[c])
        pos = pos_all[2 * c:2 * c + 2, :]
        tops = [level_scr[c, side, 0:2, :] for side in range(2)]
        high = jnp.maximum(pos, jnp.maximum(tops[0], tops[1]))
        total = jnp.exp2(pos - high)
        for side in range(2):
            total = total + level_scr[c, side, 2:4, :] * jnp.exp2(tops[side] - high)
        lse = high + jnp.log(total) * LOG2E
        loss_ref[2 * c:2 * c + 2, :] = (lse - pos) * LN2
        alpha = jnp.exp2(stats_scr[c, quarter, 0:2, :] - lse)
        for u in range(2):
            rows = slice(c * QCH + u * TILE, c * QCH + (u + 1) * TILE)
            qs_scr[rows, :] = (q_ref[rows, :].astype(jnp.float32) * wide_column(alpha[u:u + 1, :], width)).astype(jnp.bfloat16)
        return jnp.where(zl == 0, lse[0:1, :], lse[1:2, :]), jnp.where(zl == 0, pos[0:1, :], pos[1:2, :])

    def finalize(c, lse, pos):
        drain(mirror_scr.at[c, 0], mirror_recv.at[c])
        neg = None
        for side in range(2):
            term = mirror_scr[c, side].astype(jnp.float32) * jnp.exp2(level_scr[c, side, pl.ds(zl, 1), :] - lse)
            neg = term if neg is None else neg + term
        grad = (neg + (jnp.exp2(pos - lse) - 1.0) * key_t_scr[c]) * (1.0 / TAU)
        grad_rows(c)[...] = jnp.transpose(grad).astype(jnp.bfloat16)
        for m in (2, 1) if c < relayed else (3, 2, 1):
            grads[c][m - 1].start()

    def pull(k):
        rows = slice(k * span, (k + 1) * span)
        pull_scr[rows, :] = jnp.dot(p_scr[rows, :], qs_scr[...], preferred_element_type=jnp.float32).astype(jnp.bfloat16)
        pulls[k].start()

    def renew(k):
        pulls[k].wait_recv()
        for i in range(span // BCH):
            rows = slice(k * span + i * BCH, k * span + (i + 1) * BCH)
            both = pull_scr[rows, :].astype(jnp.float32) + pull_in_scr[rows, :].astype(jnp.float32)
            fresh = bank_ref[rows, :].astype(jnp.float32) + eta * both
            fresh = fresh * lax.rsqrt(jnp.mean(fresh * fresh, axis=1, keepdims=True) + EPS)
            new_ref[rows, :] = fresh.astype(jnp.bfloat16)

    q_load.wait()
    score(0)
    weigh(0)
    score(1)
    keys_load.wait()
    pl.semaphore_wait(barrier, n)
    send_squares(0)
    send_stats(0)
    send_stats(1)
    keys_copy.start()
    weigh(1)
    score(2)
    send_squares(1)
    send_stats(2)
    weigh(2)
    score(3)
    send_squares(2)
    send_stats(3)
    labels_load.wait()
    keys_copy.wait()
    weigh(3)
    pick_keys()
    send_squares(3)
    for copy in poses:
        copy.start()
    level(0)
    combine(0)
    level(1)
    combine(1)
    level(2)
    level(3)
    combine(2)
    drain(pos_scr.at[0:3], pos_recv.at[0])
    pos_all = pos_scr[0]
    for j in range(1, 4):
        pos_all = pos_all + pos_scr[j]
    settled = [settle(0, pos_all)]
    finalize(0, *settled[0])
    settled.append(settle(1, pos_all))
    combine(3)
    finalize(1, *settled[1])
    settled += [settle(2, pos_all), settle(3, pos_all)]
    pull(0)
    pull(1)
    pull(2)
    pull(3)
    finalize(2, *settled[2])
    relay(0)
    finalize(3, *settled[3])
    renew(0)
    renew(1)
    renew(2)
    renew(3)

    drain(grad_ref.at[:, 0:qdev * 3 // 4 - relayed * TILE // 2, :], grad_recv.at[0])
    drain(stats_scr.at[:, 0:3], stats_send)
    drain(level_scr.at[:, 0], level_send)
    drain(pos_scr.at[0:3], pos_send)
    drain(square_scr, square_send)
    drain(mirror_scr.at[:, 0], mirror_send)
    drain(grad_ref.at[:, 0:qdev * 3 // 4, :], grad_send)
    drain(pull_scr, pull_send)


def fused(bank, queries, keys, labels, mask_tiles):
    n = lax.axis_size("bank")
    qdev, width = queries.shape
    bdev = bank.shape[0]
    chunks = qdev // QCH
    eta = 0.25 * (bdev * n) / (qdev * lax.axis_size("batch"))
    vmem = pl.BlockSpec(memory_space=pltpu.VMEM)
    hbm = pl.BlockSpec(memory_space=pltpu.HBM)
    dma = pltpu.SemaphoreType.DMA
    new_bank, grad, loss = pl.pallas_call(
        functools.partial(step_kernel, n, eta),
        out_shape=(
            pltpu.VMEM((bdev, width), jnp.bfloat16),
            pltpu.VMEM((2, qdev, TILE), jnp.bfloat16),
            pltpu.VMEM((n, TILE), jnp.float32),
        ),
        in_specs=[hbm] * 5,
        out_specs=(vmem, vmem, vmem),
        scratch_shapes=[
            pltpu.VMEM(mask_tiles.shape, jnp.int32),
            pltpu.VMEM((bdev, width), jnp.bfloat16),
            pltpu.VMEM((qdev, width), jnp.bfloat16),
            pltpu.VMEM((qdev, width), jnp.bfloat16),
            pltpu.VMEM((n, TILE), jnp.int32),
            pltpu.VMEM((2, bdev, QCH), jnp.float32),
            pltpu.VMEM((bdev, qdev), jnp.bfloat16),
            pltpu.VMEM((width, bdev), jnp.bfloat16),
            pltpu.VMEM((n, bdev // TILE, TILE), jnp.float32),
            pltpu.VMEM((qdev, width), jnp.bfloat16),
            pltpu.VMEM((chunks, TILE, TILE), jnp.float32),
            pltpu.VMEM((chunks, 4, 4, TILE), jnp.float32),
            pltpu.VMEM((chunks, 2, 4, TILE), jnp.float32),
            pltpu.VMEM((4, 8, TILE), jnp.float32),
            pltpu.VMEM((qdev, width), jnp.bfloat16),
            pltpu.VMEM((chunks, 4, TILE, TILE), jnp.bfloat16),
            pltpu.VMEM((chunks, 3, TILE, TILE), jnp.bfloat16),
            pltpu.VMEM((chunks, 2, TILE, TILE), jnp.bfloat16),
            pltpu.VMEM((bdev, width), jnp.bfloat16),
            pltpu.VMEM((bdev, width), jnp.bfloat16),
            dma((8,)), dma((2,)), dma((7,)),
            dma((1,)), dma((chunks,)), dma((chunks,)), dma((chunks,)), dma((chunks,)), dma((3,)), dma((4,)),
        ],
        compiler_params=pltpu.CompilerParams(
            collective_id=0, has_side_effects=True, vmem_limit_bytes=60 * 1024 * 1024
        ),
    )(mask_tiles, bank, queries, keys, labels.reshape(n, TILE))
    new_bank, query_grad, loss = finish(new_bank, grad, loss)
    return (new_bank, query_grad, loss.reshape(qdev))


def finish_kernel(bank_in, grad_in, loss_in, bank_out, grad_out, loss_out, out_scr, sems):
    qdev = grad_out.shape[0]
    steps = 4
    rows = qdev // steps
    copies = [pltpu.make_async_copy(bank_in, bank_out, sems.at[0]), pltpu.make_async_copy(loss_in, loss_out, sems.at[1])]
    for c in copies: c.start()
    for i in range(steps):
        r = slice(i * rows, (i + 1) * rows)
        out_scr[r, :TILE] = grad_in[0, r, :].astype(jnp.float32)
        out_scr[r, TILE:] = grad_in[1, r, :].astype(jnp.float32)
        copies.append(pltpu.make_async_copy(out_scr.at[r, :], grad_out.at[r, :], sems.at[2 + i]))
        copies[-1].start()
    for c in copies: c.wait()


def finish(new_bank, grad, loss):
    bdev, width = new_bank.shape
    qdev = grad.shape[1]
    hbm = pl.BlockSpec(memory_space=pltpu.HBM)
    return pl.pallas_call(
        finish_kernel,
        out_shape=(
            jax.ShapeDtypeStruct((bdev, width), jnp.bfloat16),
            jax.ShapeDtypeStruct((qdev, width), jnp.float32),
            jax.ShapeDtypeStruct(loss.shape, jnp.float32),
        ),
        in_specs=[pl.BlockSpec(memory_space=pltpu.VMEM)] * 3,
        out_specs=(hbm, hbm, hbm),
        scratch_shapes=[pltpu.VMEM((qdev, width), jnp.float32), pltpu.SemaphoreType.DMA((6,))],
        compiler_params=pltpu.CompilerParams(vmem_limit_bytes=16 * 1024 * 1024),
    )(new_bank, grad, loss)


def on_device(bank, queries, keys, labels, mask_tiles):
    n = lax.axis_size("bank")
    fits = (
        n == 8
        and queries.shape == (n * TILE, 2 * TILE)
        and bank.shape[0] % BCH == 0
        and lax.axis_size("batch") == 2
    )
    return (fused if fits else general)(bank, queries, keys, labels, mask_tiles)


def solution(mesh):
    return jax.shard_map(
        on_device,
        mesh=mesh,
        in_specs=(
            P(("parts", "bank"), None),
            P(("parts", "batch"), None),
            P(("parts", "batch"), None),
            P(("parts", "batch")),
            P("parts", None),
        ),
        out_specs=(P(("parts", "bank"), None), P(("parts", "batch"), None), P(("parts", "batch"))),
        check_vma=False,
    )
```

```python
import functools
import math

import jax
import jax.numpy as jnp
from jax import lax
from jax.experimental import pallas as pl
from jax.experimental.pallas import tpu as pltpu
from jax.sharding import PartitionSpec as P

TILE = 128


TAU = 0.12
NEG = -1e30
FLOOR = -1e29
EPS = 1e-06
LOG2E = math.log2(math.e)
LN2 = math.log(2.0)
SCALE2 = LOG2E / TAU
QCH = 256
BCH = 256
MESH = pl.DeviceIdType.MESH


def masked_scores(rows_q, rows_k, mask_rows, first):
    s = jnp.einsum("qd,kd->qk", rows_q, rows_k, preferred_element_type=jnp.float32) / TAU
    nq, nk = s.shape
    ids = first + jnp.arange(nk // TILE, dtype=jnp.int32)
    hit = jnp.any(mask_rows[:, :, None] == ids[None, None, :], axis=1)
    live = jnp.broadcast_to(
        jnp.logical_not(hit)[:, None, :, None], (nq // TILE, TILE, nk // TILE, TILE)
    ).reshape(nq, nk)
    return (jnp.where(live, s, NEG), live)


def general(bank, queries, keys, labels, mask_tiles):
    qdev = queries.shape[0]
    bdev = bank.shape[0]
    total_bank = bdev * lax.axis_size("bank")
    total_query = qdev * lax.axis_size("batch")
    eta = 0.25 * total_bank / total_query
    mine = lax.axis_index("batch")
    first = lax.axis_index("bank") * (bdev // TILE)
    all_keys = lax.all_gather(keys, "batch", axis=0, tiled=True)
    key_rows = jnp.take(all_keys, labels, axis=0)
    pos = jnp.sum(queries.astype(jnp.float32) * key_rows.astype(jnp.float32), axis=1) / TAU
    own_mask = lax.dynamic_slice_in_dim(mask_tiles, mine * (qdev // TILE), qdev // TILE, 0)
    scores, live = masked_scores(queries, bank, own_mask, first)
    top = lax.pmax(jnp.max(scores, axis=1), "bank")
    part_sum = jnp.sum(jnp.where(live, jnp.exp(scores - top[:, None]), 0.0), axis=1)
    total = lax.psum(part_sum, "bank")
    high = jnp.maximum(top, pos)
    lse = high + jnp.log(total * jnp.exp(top - high) + jnp.exp(pos - high))
    loss = lse - pos
    probs = jnp.exp(scores - lse[:, None]).astype(jnp.bfloat16)
    neg_local = jnp.dot(probs, bank, preferred_element_type=jnp.float32)
    own_pull = jnp.einsum("qk,qd->kd", probs, queries, preferred_element_type=jnp.float32)
    neg = lax.psum(neg_local, "bank")
    query_grad = (neg + (jnp.exp(pos - lse) - 1.0)[:, None] * key_rows.astype(jnp.float32)) / TAU
    pull = lax.psum(own_pull.astype(jnp.bfloat16), "batch").astype(jnp.float32)
    fresh = bank.astype(jnp.float32) + eta * pull
    fresh = fresh * lax.rsqrt(jnp.mean(fresh * fresh, axis=1, keepdims=True) + EPS)
    return (fresh.astype(jnp.bfloat16), query_grad, loss)


def column(row):
    return jnp.transpose(jnp.broadcast_to(row, (TILE, TILE)))


def wide_column(row, width):
    return jnp.concatenate([column(row)] * (width // TILE), axis=1)


def step_kernel(
    n, eta, mask_hbm, bank_hbm, q_hbm, keys_hbm, labels_hbm,
    new_ref, grad_ref, loss_ref,
    mask_ref, bank_ref, q_ref, keys_ref, labels_ref,
    s_scr, p_scr, bankt_scr, bias_scr, keys_scr, key_t_scr, stats_scr, level_scr, pos_scr, qs_scr,
    stage_scr, square_scr, mirror_scr, pull_scr, pull_in_scr,
    in_sems, keys_sems, send_sems, pos_recv, stats_recv, level_recv, square_recv, mirror_recv, grad_recv, pull_recv,
):
    me = lax.axis_index("bank")
    mine = lax.axis_index("batch")
    other = 1 - mine
    bdev, width = bank_ref.shape
    qdev = q_ref.shape[0]
    tiles = bdev // TILE
    chunks = qdev // QCH
    parts = bdev // BCH
    listed = mask_ref.shape[1]
    first = me * tiles
    x = lax.rem(me, 2)
    zl = lax.rem(me // 2, 2)
    zh = me // 4
    quarter = zl * 2 + x

    relayed = 1
    pieces = 2
    piece = bdev // pieces
    mask_load = pltpu.make_async_copy(mask_hbm, mask_ref, in_sems.at[0])
    q_load = pltpu.make_async_copy(q_hbm, q_ref, in_sems.at[1])
    bank_loads = [
        pltpu.make_async_copy(bank_hbm.at[i * piece:(i + 1) * piece, :], bank_ref.at[i * piece:(i + 1) * piece, :], in_sems.at[4 + i])
        for i in range(pieces)]
    labels_load = pltpu.make_async_copy(labels_hbm, labels_ref, in_sems.at[2])
    keys_load = pltpu.make_async_copy(keys_hbm, keys_ref, in_sems.at[3])
    for load in [mask_load, q_load] + bank_loads + [labels_load, keys_load]:
        load.start()

    barrier = pltpu.get_barrier_semaphore()
    for d in range(1, n):
        pl.semaphore_signal(barrier, inc=1, device_id={"bank": lax.rem(me + d, n)}, device_id_type=MESH)
    pl.semaphore_signal(barrier, inc=1, device_id={"batch": other}, device_id_type=MESH)

    def peer(m):
        low = (1 - zl if m & 2 else zl) * 2 + (1 - x if m & 1 else x)
        return low, (1 - zh if m & 4 else zh) * 4 + low

    def to_bank(m, src, dst, send, recv):
        return pltpu.make_async_remote_copy(
            src_ref=src, dst_ref=dst, send_sem=send, recv_sem=recv,
            device_id={"bank": peer(m)[1]}, device_id_type=MESH)

    def to_core(src, dst, send, recv):
        return pltpu.make_async_remote_copy(
            src_ref=src, dst_ref=dst, send_sem=send, recv_sem=recv,
            device_id={"batch": other}, device_id_type=MESH)

    keys_copy = to_core(keys_ref, keys_scr, keys_sems.at[0], keys_sems.at[1])
    def drain(ref, sem):
        pltpu.make_async_copy(ref, ref, sem).wait()

    stats_send, level_send, pos_send, square_send, mirror_send, grad_send, pull_send = [send_sems.at[i] for i in range(7)]
    stats = [[to_bank(m, stats_scr.at[c, quarter], stats_scr.at[c, quarter], stats_send, stats_recv.at[c])
              for m in range(1, 4)] for c in range(chunks)]
    levels = [to_bank(4, level_scr.at[c, zh], level_scr.at[c, zh], level_send, level_recv.at[c]) for c in range(chunks)]
    poses = [to_bank(m, pos_scr.at[quarter], pos_scr.at[quarter], pos_send, pos_recv.at[0]) for m in range(1, 4)]
    squares = [[to_bank(m, stage_scr.at[c, peer(m)[0]], square_scr.at[c, m - 1], square_send, square_recv.at[c])
                for m in range(1, 4)] for c in range(chunks)]
    mirrors = [to_bank(4, mirror_scr.at[c, zh], mirror_scr.at[c, zh], mirror_send, mirror_recv.at[c]) for c in range(chunks)]

    def grad_rows(c):
        return grad_ref.at[x, pl.ds(pl.multiple_of(c * QCH + zl * TILE, TILE), TILE), :]

    grads = [[to_bank(m, grad_rows(c), grad_rows(c), grad_send, grad_recv.at[1 + c if m == 2 and c < relayed else 0])
              for m in range(1, 4)] for c in range(chunks)]

    def came_rows(c):
        return grad_ref.at[x, pl.ds(pl.multiple_of(c * QCH + (1 - zl) * TILE, TILE), TILE), :]

    relays = [to_bank(1, came_rows(c), came_rows(c), grad_send, grad_recv.at[0]) for c in range(relayed)]

    def relay(c):
        drain(came_rows(c), grad_recv.at[1 + c])
        relays[c].start()
    sends = 4
    span = bdev // sends
    pulls = [to_core(pull_scr.at[k * span:(k + 1) * span, :], pull_in_scr.at[k * span:(k + 1) * span, :], pull_send, pull_recv.at[k])
             for k in range(sends)]

    mask_load.wait()
    ids = first + lax.broadcasted_iota(jnp.int32, (tiles, listed), 0)
    for b in range(qdev // TILE):
        hit = jnp.where(ids == mask_ref[pl.ds(mine * (qdev // TILE) + b, 1), :], 1.0, 0.0)
        bias_scr[b] = jnp.broadcast_to(jnp.max(hit, axis=1, keepdims=True), (tiles, TILE)) * NEG

    def score(c):
        cols = slice(c * QCH, (c + 1) * QCH)
        bias = [jnp.concatenate([bias_scr[c * (QCH // TILE) + u, t:t + 1, :] for u in range(QCH // TILE)], axis=1) for t in range(tiles)]
        qc = q_ref[cols, :]
        top8 = jnp.full((8, QCH), FLOOR / SCALE2, jnp.float32)
        for k in range(parts):
            if c == 0 and k * BCH % piece == 0:
                bank_loads[k * BCH // piece].wait()
            s = lax.dot_general(bank_ref[k * BCH:(k + 1) * BCH, :], qc, (((1,), (1,)), ((), ())),
                                preferred_element_type=jnp.float32)
            s_scr[c % 2, k * BCH:(k + 1) * BCH, :] = s
            for t in range(BCH // TILE):
                part = s[t * TILE:(t + 1) * TILE, :].reshape(TILE // 8, 8, QCH)
                top8 = jnp.maximum(top8, jnp.max(part, axis=0) + bias[k * (BCH // TILE) + t])
            if c == 0:
                bankt_scr[:, k * BCH:(k + 1) * BCH] = jnp.transpose(bank_ref[k * BCH:(k + 1) * BCH, :])
        top = jnp.max(top8, axis=0, keepdims=True) * SCALE2
        sum8 = jnp.zeros((8, QCH), jnp.float32)
        for t in range(tiles):
            rows = slice(t * TILE, (t + 1) * TILE)
            p = jnp.exp2(s_scr[c % 2, rows, :] * SCALE2 - (top - bias[t]))
            sum8 = sum8 + jnp.sum(p.reshape(TILE // 8, 8, QCH), axis=0)
            p_scr[rows, cols] = p.astype(jnp.bfloat16)
        total = jnp.sum(sum8, axis=0, keepdims=True)
        for u in range(QCH // TILE):
            stats_scr[c, quarter, u:u + 1, :] = top[:, u * TILE:(u + 1) * TILE]
            stats_scr[c, quarter, 2 + u:3 + u, :] = total[:, u * TILE:(u + 1) * TILE]

    def weigh(c):
        cols = slice(c * QCH, (c + 1) * QCH)
        neg = jnp.dot(bankt_scr[...], p_scr[:, cols], preferred_element_type=jnp.float32).astype(jnp.bfloat16)
        for u in range(2):
            for h in range(2):
                stage_scr[c, u * 2 + h] = neg[h * TILE:(h + 1) * TILE, u * TILE:(u + 1) * TILE]

    def send_stats(c):
        for copy in stats[c]:
            copy.start()

    def send_squares(c):
        for m in (3, 2, 1):
            squares[c][m - 1].start()

    def pick_keys():
        half = pl.ds(pl.multiple_of(x * TILE, TILE), TILE)
        row_ids = lax.broadcasted_iota(jnp.int32, (qdev, TILE), 0)
        row8 = lax.broadcasted_iota(jnp.int32, (8, TILE), 0)

        def picked(table, labels):
            hot = jnp.where(row_ids == labels, 1.0, 0.0).astype(jnp.bfloat16)
            return lax.dot_general(hot, table, (((0,), (0,)), ((), ())), preferred_element_type=jnp.float32)

        tile = jnp.zeros((8, TILE), jnp.float32)
        for c in range(chunks):
            labels = labels_ref[pl.ds(2 * c + zl, 1), :]
            rows = picked(keys_ref[:, half], labels - mine * qdev) + picked(keys_scr[:, half], labels - other * qdev)
            key_t = jnp.transpose(rows)
            key_t_scr[c] = key_t
            own = pl.ds(pl.multiple_of(c * QCH + zl * TILE, TILE), TILE)
            q_t = jnp.transpose(q_ref[own, half].astype(jnp.float32))
            pos = jnp.sum(key_t * q_t, axis=0, keepdims=True) * SCALE2
            tile = jnp.where(row8 == 2 * c + zl, pos, tile)
        pos_scr[quarter] = tile

    def level(c):
        drain(stats_scr.at[c, 0:3], stats_recv.at[c])
        top = stats_scr[c, 0, 0:2, :]
        for b in range(1, 4):
            top = jnp.maximum(top, stats_scr[c, b, 0:2, :])
        total = stats_scr[c, 0, 2:4, :] * jnp.exp2(stats_scr[c, 0, 0:2, :] - top)
        for b in range(1, 4):
            total = total + stats_scr[c, b, 2:4, :] * jnp.exp2(stats_scr[c, b, 0:2, :] - top)
        level_scr[c, zh, 0:2, :] = top
        level_scr[c, zh, 2:4, :] = total
        levels[c].start()

    def combine(c):
        drain(square_scr.at[c], square_recv.at[c])
        both = level_scr[c, zh, pl.ds(zl, 1), :]
        total = None
        for m in range(4):
            piece = stage_scr[c, quarter] if m == 0 else square_scr[c, m - 1]
            term = piece.astype(jnp.float32) * jnp.exp2(stats_scr[c, peer(m)[0], pl.ds(zl, 1), :] - both)
            total = term if m == 0 else total + term
        mirror_scr[c, zh] = total.astype(jnp.bfloat16)
        mirrors[c].start()

    def settle(c, pos_all):
        drain(level_scr.at[c, 0], level_recv.at[c])
        pos = pos_all[2 * c:2 * c + 2, :]
        tops = [level_scr[c, side, 0:2, :] for side in range(2)]
        high = jnp.maximum(pos, jnp.maximum(tops[0], tops[1]))
        total = jnp.exp2(pos - high)
        for side in range(2):
            total = total + level_scr[c, side, 2:4, :] * jnp.exp2(tops[side] - high)
        lse = high + jnp.log(total) * LOG2E
        loss_ref[2 * c:2 * c + 2, :] = (lse - pos) * LN2
        alpha = jnp.exp2(stats_scr[c, quarter, 0:2, :] - lse)
        for u in range(2):
            rows = slice(c * QCH + u * TILE, c * QCH + (u + 1) * TILE)
            qs_scr[rows, :] = (q_ref[rows, :].astype(jnp.float32) * wide_column(alpha[u:u + 1, :], width)).astype(jnp.bfloat16)
        return jnp.where(zl == 0, lse[0:1, :], lse[1:2, :]), jnp.where(zl == 0, pos[0:1, :], pos[1:2, :])

    def finalize(c, lse, pos):
        drain(mirror_scr.at[c, 0], mirror_recv.at[c])
        neg = None
        for side in range(2):
            term = mirror_scr[c, side].astype(jnp.float32) * jnp.exp2(level_scr[c, side, pl.ds(zl, 1), :] - lse)
            neg = term if neg is None else neg + term
        grad = (neg + (jnp.exp2(pos - lse) - 1.0) * key_t_scr[c]) * (1.0 / TAU)
        grad_rows(c)[...] = jnp.transpose(grad).astype(jnp.bfloat16)
        for m in (2, 1) if c < relayed else (3, 2, 1):
            grads[c][m - 1].start()

    def pull(k):
        rows = slice(k * span, (k + 1) * span)
        pull_scr[rows, :] = jnp.dot(p_scr[rows, :], qs_scr[...], preferred_element_type=jnp.float32).astype(jnp.bfloat16)
        pulls[k].start()

    def renew(k):
        pulls[k].wait_recv()
        for i in range(span // BCH):
            rows = slice(k * span + i * BCH, k * span + (i + 1) * BCH)
            both = pull_scr[rows, :].astype(jnp.float32) + pull_in_scr[rows, :].astype(jnp.float32)
            fresh = bank_ref[rows, :].astype(jnp.float32) + eta * both
            fresh = fresh * lax.rsqrt(jnp.mean(fresh * fresh, axis=1, keepdims=True) + EPS)
            new_ref[rows, :] = fresh.astype(jnp.bfloat16)

    q_load.wait()
    score(0)
    weigh(0)
    score(1)
    keys_load.wait()
    pl.semaphore_wait(barrier, n)
    send_squares(0)
    send_stats(0)
    send_stats(1)
    keys_copy.start()
    weigh(1)
    score(2)
    send_squares(1)
    send_stats(2)
    weigh(2)
    score(3)
    send_squares(2)
    send_stats(3)
    labels_load.wait()
    keys_copy.wait()
    weigh(3)
    pick_keys()
    send_squares(3)
    for copy in poses:
        copy.start()
    level(0)
    combine(0)
    level(1)
    combine(1)
    level(2)
    level(3)
    combine(2)
    drain(pos_scr.at[0:3], pos_recv.at[0])
    pos_all = pos_scr[0]
    for j in range(1, 4):
        pos_all = pos_all + pos_scr[j]
    settled = [settle(0, pos_all)]
    finalize(0, *settled[0])
    settled.append(settle(1, pos_all))
    combine(3)
    finalize(1, *settled[1])
    settled += [settle(2, pos_all), settle(3, pos_all)]
    pull(0)
    pull(1)
    pull(2)
    pull(3)
    finalize(2, *settled[2])
    finalize(3, *settled[3])
    relay(0)
    renew(0)
    renew(1)
    renew(2)
    renew(3)

    drain(grad_ref.at[:, 0:qdev * 3 // 4 - relayed * TILE // 2, :], grad_recv.at[0])
    drain(stats_scr.at[:, 0:3], stats_send)
    drain(level_scr.at[:, 0], level_send)
    drain(pos_scr.at[0:3], pos_send)
    drain(square_scr, square_send)
    drain(mirror_scr.at[:, 0], mirror_send)
    drain(grad_ref.at[:, 0:qdev * 3 // 4, :], grad_send)
    drain(pull_scr, pull_send)


def fused(bank, queries, keys, labels, mask_tiles):
    n = lax.axis_size("bank")
    qdev, width = queries.shape
    bdev = bank.shape[0]
    chunks = qdev // QCH
    eta = 0.25 * (bdev * n) / (qdev * lax.axis_size("batch"))
    vmem = pl.BlockSpec(memory_space=pltpu.VMEM)
    hbm = pl.BlockSpec(memory_space=pltpu.HBM)
    dma = pltpu.SemaphoreType.DMA
    new_bank, grad, loss = pl.pallas_call(
        functools.partial(step_kernel, n, eta),
        out_shape=(
            pltpu.VMEM((bdev, width), jnp.bfloat16),
            pltpu.VMEM((2, qdev, TILE), jnp.bfloat16),
            pltpu.VMEM((n, TILE), jnp.float32),
        ),
        in_specs=[hbm] * 5,
        out_specs=(vmem, vmem, vmem),
        scratch_shapes=[
            pltpu.VMEM(mask_tiles.shape, jnp.int32),
            pltpu.VMEM((bdev, width), jnp.bfloat16),
            pltpu.VMEM((qdev, width), jnp.bfloat16),
            pltpu.VMEM((qdev, width), jnp.bfloat16),
            pltpu.VMEM((n, TILE), jnp.int32),
            pltpu.VMEM((2, bdev, QCH), jnp.float32),
            pltpu.VMEM((bdev, qdev), jnp.bfloat16),
            pltpu.VMEM((width, bdev), jnp.bfloat16),
            pltpu.VMEM((n, bdev // TILE, TILE), jnp.float32),
            pltpu.VMEM((qdev, width), jnp.bfloat16),
            pltpu.VMEM((chunks, TILE, TILE), jnp.float32),
            pltpu.VMEM((chunks, 4, 4, TILE), jnp.float32),
            pltpu.VMEM((chunks, 2, 4, TILE), jnp.float32),
            pltpu.VMEM((4, 8, TILE), jnp.float32),
            pltpu.VMEM((qdev, width), jnp.bfloat16),
            pltpu.VMEM((chunks, 4, TILE, TILE), jnp.bfloat16),
            pltpu.VMEM((chunks, 3, TILE, TILE), jnp.bfloat16),
            pltpu.VMEM((chunks, 2, TILE, TILE), jnp.bfloat16),
            pltpu.VMEM((bdev, width), jnp.bfloat16),
            pltpu.VMEM((bdev, width), jnp.bfloat16),
            dma((8,)), dma((2,)), dma((7,)),
            dma((1,)), dma((chunks,)), dma((chunks,)), dma((chunks,)), dma((chunks,)), dma((3,)), dma((4,)),
        ],
        compiler_params=pltpu.CompilerParams(
            collective_id=0, has_side_effects=True, vmem_limit_bytes=60 * 1024 * 1024
        ),
    )(mask_tiles, bank, queries, keys, labels.reshape(n, TILE))
    new_bank, query_grad, loss = finish(new_bank, grad, loss)
    return (new_bank, query_grad, loss.reshape(qdev))


def finish_kernel(bank_in, grad_in, loss_in, bank_out, grad_out, loss_out, out_scr, sems):
    qdev = grad_out.shape[0]
    steps = 4
    rows = qdev // steps
    copies = [pltpu.make_async_copy(bank_in, bank_out, sems.at[0]), pltpu.make_async_copy(loss_in, loss_out, sems.at[1])]
    for c in copies: c.start()
    for i in range(steps):
        r = slice(i * rows, (i + 1) * rows)
        out_scr[r, :TILE] = grad_in[0, r, :].astype(jnp.float32)
        out_scr[r, TILE:] = grad_in[1, r, :].astype(jnp.float32)
        copies.append(pltpu.make_async_copy(out_scr.at[r, :], grad_out.at[r, :], sems.at[2 + i]))
        copies[-1].start()
    for c in copies: c.wait()


def finish(new_bank, grad, loss):
    bdev, width = new_bank.shape
    qdev = grad.shape[1]
    hbm = pl.BlockSpec(memory_space=pltpu.HBM)
    return pl.pallas_call(
        finish_kernel,
        out_shape=(
            jax.ShapeDtypeStruct((bdev, width), jnp.bfloat16),
            jax.ShapeDtypeStruct((qdev, width), jnp.float32),
            jax.ShapeDtypeStruct(loss.shape, jnp.float32),
        ),
        in_specs=[pl.BlockSpec(memory_space=pltpu.VMEM)] * 3,
        out_specs=(hbm, hbm, hbm),
        scratch_shapes=[pltpu.VMEM((qdev, width), jnp.float32), pltpu.SemaphoreType.DMA((6,))],
        compiler_params=pltpu.CompilerParams(vmem_limit_bytes=16 * 1024 * 1024),
    )(new_bank, grad, loss)


def on_device(bank, queries, keys, labels, mask_tiles):
    n = lax.axis_size("bank")
    fits = (
        n == 8
        and queries.shape == (n * TILE, 2 * TILE)
        and bank.shape[0] % BCH == 0
        and lax.axis_size("batch") == 2
    )
    return (fused if fits else general)(bank, queries, keys, labels, mask_tiles)


def solution(mesh):
    return jax.shard_map(
        on_device,
        mesh=mesh,
        in_specs=(
            P(("parts", "bank"), None),
            P(("parts", "batch"), None),
            P(("parts", "batch"), None),
            P(("parts", "batch")),
            P("parts", None),
        ),
        out_specs=(P(("parts", "bank"), None), P(("parts", "batch"), None), P(("parts", "batch"))),
        check_vma=False,
    )
```
